512 devices in a mesh: dp: 16 (over z), ctx: 32 (over x, y, core).
Axes of the slice: x: 4, y: 4, z: 16, core: 2. Of those that a mesh axis runs over, the one named last changes fastest.
Arguments:
- tokens: bfloat16 [16, 8192, 1024], P('dp', 'ctx'), may hold values from -14 to 14
- w_query: bfloat16 [1024, 1024], replicated, may hold values from -0.1875 to 0.1875
- key_weight: bfloat16 [1024, 256], replicated, may hold values from -0.1875 to 0.1875
- value_weight: bfloat16 [1024, 256], replicated, may hold values from -0.1875 to 0.1875
- cotangent: bfloat16 [16, 8192, 1024], P('dp', 'ctx'), may hold values from -6 to 6
- segment_ids: int32 [16, 8192], P('dp'), may hold values from 0 to 3, never falling along the last dimension, each value on 1 to 4096 neighbouring positions
Outputs:
- grad_inputs: bfloat16 [16, 8192, 1024], P('dp', 'ctx')
- grad_query: float32 [1024, 1024], P('ctx')
- key_weight_gradient: float32 [1024, 256], P('ctx')
- value_weight_gradient: float32 [1024, 256], P('ctx')
The draws below stay inside these ranges and needn't reach their ends.
Inputs may be any that keep to these rules, and one draw needn't show every extreme that they name: `segment_ids`: along each sequence the document numbers never fall and start at 0; each document has 1 to min(4096, 6144) bytes, and one has exactly that many.
All inputs are finite; a program needn't handle non-finite values.
Results may differ from the reference program's by a relative error of at most 0.014.
The reference program's roundings to bfloat16 on the way count: a program that leaves them out, or rounds other values in their place, can miss the bound.
Values may be sent and summed in bfloat16 or wider, within the bound.
A program may use at most 64 MiB of HBM per device.

```python
import math
import jax
import jax.numpy as jnp
import numpy as np
from jax import lax

MODEL_WIDTH = 1024
QUERY_HEADS = 8
KEY_VALUE_HEADS = 2
HEAD_DIMENSION = 128
TOK_DEV = 256
WINDOW = 1024
LENGTH = 8192
BATCH = 16


def draw_tokens(key, part):
    base_key = jax.random.fold_in(jax.random.fold_in(key, 11), 0)
    shape = (BATCH, LENGTH, MODEL_WIDTH)
    values = jnp.clip(jax.random.normal(base_key, shape, jnp.float32), -6.0, 6.0)
    return values.astype(jnp.bfloat16)


def steps_of(stream_key, shape, pieces, least, high):
    def one(axis_at, parts):
        heights = jax.random.uniform(jax.random.fold_in(jax.random.fold_in(stream_key, 6), axis_at), (parts,), jnp.float32, least / len(pieces), high / len(pieces))
        return jnp.repeat(jnp.exp(heights), shape[axis_at] // parts).reshape((-1,) + (1,) * (len(shape) - axis_at - 1))

    loudness = one(*pieces[0])
    for cut in pieces[1:]:
        loudness = loudness * one(*cut)
    return loudness


def profile(count, total, reach, slope):
    loads = [(1 << 20) // math.isqrt(rank ** slope) + 1 for rank in range(2, count + 1)]
    spare, holding = total - reach - (count - 1), [1] * (count - 1)
    while spare > 0:
        free = [i for i in range(count - 1) if holding[i] < reach]
        pool, remaining = sum([loads[i] for i in free]), spare
        for i in free:
            more = min(reach - holding[i], max(1, remaining * loads[i] // pool), spare)
            holding[i] = holding[i] + more
            spare = spare - more
    return np.array([reach] + holding)


def uneven_parts(key, amount, total, reach, skew):
    if amount == 2:
        one = jax.random.randint(key, (), max(1, total - reach), min(reach, total - 1) + 1)
        return jnp.stack([one, total - one])
    tallies = jnp.asarray(profile(amount, total, reach, skew), jnp.int32)
    couples = (amount - 1) // 2
    donor, taker = tallies[1:1 + 2 * couples:2], tallies[2:2 + 2 * couples:2]
    slack = jnp.minimum(donor - 1, reach - taker)
    passed = jax.random.randint(jax.random.fold_in(key, 1), (couples,), 0, 1 << 20) % (slack + 1)
    tallies = tallies.at[1:1 + 2 * couples:2].set(donor - passed).at[2:2 + 2 * couples:2].set(taker + passed)
    return tallies[jax.random.permutation(jax.random.fold_in(key, 2), amount)]


def gaussian(key, extent, scale, most, pieces=(), kind=jnp.bfloat16):
    entries = scale * jax.random.normal(key, extent, jnp.float32)
    if pieces:
        entries = entries * steps_of(key, extent, pieces, -0.22, 0.18)
    return jnp.clip(entries, -most, most).astype(kind)


def setup_inputs(seed: int = 0) -> dict:
    streams_of = jax.random.split(jax.random.key(seed), 7)
    tokens = draw_tokens(jax.random.fold_in(streams_of[6], 71), 0)
    w_query = gaussian(streams_of[1], (MODEL_WIDTH, QUERY_HEADS * HEAD_DIMENSION), MODEL_WIDTH ** -0.5, 0.1875)
    key_weight = gaussian(streams_of[2], (MODEL_WIDTH, KEY_VALUE_HEADS * HEAD_DIMENSION), MODEL_WIDTH ** -0.5, 0.1875)
    value_weight = gaussian(streams_of[3], (MODEL_WIDTH, KEY_VALUE_HEADS * HEAD_DIMENSION), MODEL_WIDTH ** -0.5, 0.1875)
    cotangent = gaussian(streams_of[4], (BATCH, LENGTH, QUERY_HEADS * HEAD_DIMENSION), 1.0, 6.0, ((0, 16), (1, 32)))
    segment_ids = jax.vmap(lambda own: jnp.searchsorted(jnp.cumsum(uneven_parts(own, max(2, LENGTH // (2 * WINDOW)), LENGTH, min(4 * WINDOW, (3 * LENGTH) // 4), 1)), jnp.arange(LENGTH), side="right"))(jax.random.split(streams_of[5], BATCH)).reshape((BATCH, LENGTH)).astype(jnp.int32)
    return {"tokens": tokens, "w_query": w_query, "key_weight": key_weight, "value_weight": value_weight, "cotangent": cotangent, "segment_ids": segment_ids}


NEG_FILL = -1e30


def head_terms(head_index, q_block, k_block, v_block, c_block, allowed, scale):
    query_group = head_index // (QUERY_HEADS // KEY_VALUE_HEADS)
    query = lax.dynamic_slice_in_dim(q_block, head_index * HEAD_DIMENSION, HEAD_DIMENSION, 1)
    key_h = lax.dynamic_slice_in_dim(k_block, query_group * HEAD_DIMENSION, HEAD_DIMENSION, 1)
    value_h = lax.dynamic_slice_in_dim(v_block, query_group * HEAD_DIMENSION, HEAD_DIMENSION, 1)
    dout = lax.dynamic_slice_in_dim(c_block, head_index * HEAD_DIMENSION, HEAD_DIMENSION, 1)
    scores = jnp.dot(query, key_h.T, preferred_element_type=jnp.float32) * scale
    scores = jnp.where(allowed, scores, NEG_FILL)
    peak = jnp.max(scores, axis=1, keepdims=True)
    weights = jnp.exp(scores - peak)
    weights = weights / jnp.sum(weights, axis=1, keepdims=True)
    weights_b = weights.astype(jnp.bfloat16)
    attended = jnp.dot(weights_b, value_h, preferred_element_type=jnp.float32)
    delta = jnp.sum(dout.astype(jnp.float32) * attended, axis=1, keepdims=True)
    dprobs = jnp.dot(dout, value_h.T, preferred_element_type=jnp.float32)
    dscores = (weights * (dprobs - delta) * scale).astype(jnp.bfloat16)
    grad_q = jnp.dot(dscores, key_h, preferred_element_type=jnp.float32)
    key_gradient = jnp.dot(dscores.T, query, preferred_element_type=jnp.float32)
    value_gradient = jnp.dot(weights_b.T, dout, preferred_element_type=jnp.float32)
    return grad_q, key_gradient, value_gradient


def one_sequence(sequence, cot, seg, w_query, key_weight, value_weight):
    scale = HEAD_DIMENSION ** -0.5
    column_width = WINDOW + TOK_DEV
    key_value_columns = KEY_VALUE_HEADS * HEAD_DIMENSION
    queries = jnp.dot(sequence, w_query, preferred_element_type=jnp.float32).astype(jnp.bfloat16)
    keys = jnp.dot(sequence, key_weight, preferred_element_type=jnp.float32).astype(jnp.bfloat16)
    values = jnp.dot(sequence, value_weight, preferred_element_type=jnp.float32).astype(jnp.bfloat16)
    filler = jnp.zeros((WINDOW, key_value_columns), jnp.bfloat16)
    keys_pad = jnp.concatenate([filler, keys], axis=0)
    values_pad = jnp.concatenate([filler, values], axis=0)
    seg_pad = jnp.concatenate([-jnp.ones((WINDOW,), jnp.int32), seg.astype(jnp.int32)], axis=0)
    block_list = LENGTH // TOK_DEV

    def step(carry, index):
        dk_acc, dv_acc = carry
        start = (index * TOK_DEV).astype(jnp.int32)
        q_block = lax.dynamic_slice_in_dim(queries, start, TOK_DEV, 0)
        c_block = lax.dynamic_slice_in_dim(cot, start, TOK_DEV, 0)
        k_block = lax.dynamic_slice_in_dim(keys_pad, start, column_width, 0)
        v_block = lax.dynamic_slice_in_dim(values_pad, start, column_width, 0)
        q_seg = lax.dynamic_slice_in_dim(seg, start, TOK_DEV, 0)
        k_seg = lax.dynamic_slice_in_dim(seg_pad, start, column_width, 0)
        q_pos = start + jnp.arange(TOK_DEV, dtype=jnp.int32)
        k_pos = start - WINDOW + jnp.arange(column_width, dtype=jnp.int32)
        gap = q_pos[:, None] - k_pos[None, :]
        allowed = (gap >= 0) & (gap < WINDOW) & (k_pos[None, :] >= 0) & (q_seg[:, None] == k_seg[None, :])
        grad_q, key_gradient, value_gradient = lax.map(
            lambda head_index: head_terms(head_index, q_block, k_block, v_block, c_block, allowed, scale),
            jnp.arange(QUERY_HEADS, dtype=jnp.int32))
        dq_block = grad_q.transpose(1, 0, 2).reshape(TOK_DEV, QUERY_HEADS * HEAD_DIMENSION).astype(jnp.bfloat16)
        key_grad_sum = key_gradient.reshape(KEY_VALUE_HEADS, QUERY_HEADS // KEY_VALUE_HEADS, column_width, HEAD_DIMENSION).sum(axis=1).transpose(1, 0, 2).reshape(column_width, key_value_columns)
        value_grad_sum = value_gradient.reshape(KEY_VALUE_HEADS, QUERY_HEADS // KEY_VALUE_HEADS, column_width, HEAD_DIMENSION).sum(axis=1).transpose(1, 0, 2).reshape(column_width, key_value_columns)
        dk_acc = lax.dynamic_update_slice_in_dim(dk_acc, lax.dynamic_slice_in_dim(dk_acc, start, column_width, 0) + key_grad_sum, start, 0)
        dv_acc = lax.dynamic_update_slice_in_dim(dv_acc, lax.dynamic_slice_in_dim(dv_acc, start, column_width, 0) + value_grad_sum, start, 0)
        return (dk_acc, dv_acc), dq_block

    zeros_acc = jnp.zeros((LENGTH + WINDOW, key_value_columns), jnp.float32)
    (dk_acc, dv_acc), dq_blocks = lax.scan(step, (zeros_acc, zeros_acc), jnp.arange(block_list, dtype=jnp.int32))
    grad_q = dq_blocks.reshape(LENGTH, QUERY_HEADS * HEAD_DIMENSION)
    key_gradient = dk_acc[WINDOW:].astype(jnp.bfloat16)
    value_gradient = dv_acc[WINDOW:].astype(jnp.bfloat16)
    grad_in = (jnp.dot(grad_q, w_query.T, preferred_element_type=jnp.float32)
               + jnp.dot(key_gradient, key_weight.T, preferred_element_type=jnp.float32)
               + jnp.dot(value_gradient, value_weight.T, preferred_element_type=jnp.float32)).astype(jnp.bfloat16)
    combined = jnp.concatenate([grad_q, key_gradient, value_gradient], axis=1)

    def weight_update(grand_total, index):
        start = (index * TOK_DEV).astype(jnp.int32)
        run_in = lax.dynamic_slice_in_dim(sequence, start, TOK_DEV, 0)
        run_grad = lax.dynamic_slice_in_dim(combined, start, TOK_DEV, 0)
        partial_value = lax.dot_general(run_in, run_grad, (((0,), (0,)), ((), ())), preferred_element_type=jnp.float32)
        rounded = lax.optimization_barrier(partial_value.astype(jnp.bfloat16)).astype(jnp.float32)
        return grand_total + rounded, None

    grand_total, unused_item = lax.scan(weight_update, jnp.zeros((MODEL_WIDTH, (QUERY_HEADS + 2 * KEY_VALUE_HEADS) * HEAD_DIMENSION), jnp.float32), jnp.arange(block_list, dtype=jnp.int32))
    return grad_in, grand_total


def reference(tokens, w_query, key_weight, value_weight, cotangent, segment_ids):
    def per_sequence(items):
        return one_sequence(items[0], items[1], items[2], w_query, key_weight, value_weight)

    grad_inputs, totals = lax.map(per_sequence, (tokens, cotangent, segment_ids))
    grand_total = jnp.sum(totals, axis=0) * ((BATCH * LENGTH) ** -0.5)
    grad_query = grand_total[:, :QUERY_HEADS * HEAD_DIMENSION]
    key_weight_gradient = grand_total[:, QUERY_HEADS * HEAD_DIMENSION:QUERY_HEADS * HEAD_DIMENSION + KEY_VALUE_HEADS * HEAD_DIMENSION]
    value_weight_gradient = grand_total[:, QUERY_HEADS * HEAD_DIMENSION + KEY_VALUE_HEADS * HEAD_DIMENSION:]
    return grad_inputs, grad_query, key_weight_gradient, value_weight_gradient
```

```python
import functools
import math

import jax
import jax.numpy as jnp
from jax import lax
from jax.experimental import pallas as pl
from jax.experimental.pallas import tpu as pltpu
from jax.sharding import PartitionSpec as P

HEAD = 128
WINDOW = 1024
NEG = -1e30
BF = jnp.bfloat16
F32 = jnp.float32
MESH = pl.DeviceIdType.MESH


def nn(a, b):
    return lax.dot_general(a, b, (((1,), (0,)), ((), ())), preferred_element_type=F32)


def nt(a, b):
    return lax.dot_general(a, b, (((1,), (1,)), ((), ())), preferred_element_type=F32)


def tn(a, b):
    return lax.dot_general(a, b, (((0,), (0,)), ((), ())), preferred_element_type=F32)


class Plan:
    def __init__(self, sizes, rows, width, q_cols, kv_cols, length):
        self.Z, self.N = sizes["dp"], sizes["ctx"]
        self.X = self.Y = math.isqrt(self.N // 2)
        self.rows, self.width, self.q_cols, self.kv_cols = rows, width, q_cols, kv_cols
        self.length = length
        self.heads = q_cols // HEAD
        self.groups = kv_cols // HEAD
        self.per = self.heads // self.groups
        self.reach = WINDOW // rows
        self.chips = self.N // 2
        self.own = width // self.N
        half = q_cols // 2
        self.q_pieces = ((0, half, True), (half, half, False))
        self.kv_pieces = ((q_cols, kv_cols, True), (q_cols + kv_cols, kv_cols, False))
        self.parts = (self.q_pieces, self.kv_pieces)
        self.scratch = {}
        self.sems = {}

    def buf(self, name, shape, dtype):
        self.scratch[name] = pltpu.VMEM(shape, dtype)

    def sem(self, name, *shape):
        self.sems[name] = pltpu.SemaphoreType.DMA(shape)


def build_plan(sizes, rows, width, q_cols, kv_cols, length):
    p = Plan(sizes, rows, width, q_cols, kv_cols, length)
    lanes = p.per * rows
    blocks = p.reach + 1
    p.buf("tok", (rows, width), BF)
    p.buf("wq", (width, q_cols), BF)
    p.buf("wk", (width, kv_cols), BF)
    p.buf("wv", (width, kv_cols), BF)
    p.buf("cot", (rows, q_cols), BF)
    p.buf("seg", (1, length), jnp.int32)
    p.buf("kvb", (blocks, 2 * p.groups, rows, HEAD), BF)
    p.buf("qst", (p.groups, lanes, HEAD), BF)
    p.buf("dost", (p.groups, lanes, HEAD), BF)
    p.buf("bias", (blocks, rows, rows), F32)
    p.buf("s", (p.groups, blocks, rows, lanes), F32)
    p.buf("dp", (p.groups, blocks, rows, lanes), F32)
    p.buf("m", (p.groups, 8, lanes), F32)
    p.buf("l", (8, lanes), F32)
    p.buf("de", (8, lanes), F32)
    p.buf("acc", (p.groups, blocks, 2, rows, HEAD), F32)
    p.buf("dqt", (HEAD, lanes), F32)
    p.buf("stage", (p.groups, blocks, 2, rows, HEAD), BF)
    p.buf("back", (p.groups, blocks, 2, rows, HEAD), BF)
    p.buf("tokt", (2, width // 2, rows), BF)
    p.buf("toktp", (width // 2, rows), BF)
    p.buf("dq", (rows, q_cols), BF)
    p.buf("dqp", (rows, q_cols), BF)
    p.buf("dkv", (2, rows, kv_cols), BF)
    p.buf("dkvp", (2, rows, kv_cols), BF)
    p.buf("gi32", (rows, width), F32)
    p.buf("gi", (rows, width), BF)
    own, R = p.own, p.X
    for i, part in enumerate(p.parts):
        for j, (first, cols, x_first) in enumerate(part):
            p.buf(f"one{i}{j}", (R, R * own, cols), BF)
            p.buf(f"got{i}{j}", (R - 1, R * own, cols), BF)
            p.buf(f"two{i}{j}", (R, own, cols), BF)
            p.buf(f"gat{i}{j}", (R - 1, own, cols), BF)
            p.sem(f"one{i}{j}", 2, R)
            p.sem(f"two{i}{j}", 2, R)
        tiles = own // 8 * sum(c for _, c, _ in part) // HEAD
        p.buf(f"zs{i}", (p.Z, tiles // p.Z * 8, HEAD), F32)
        p.buf(f"zr{i}", (p.Z, tiles // p.Z * 8, HEAD), F32)
        p.buf(f"zo{i}", (p.Z, tiles // p.Z * 8, HEAD), F32)
        p.sem(f"zr{i}", 2, p.Z)
        p.sem(f"zo{i}", 2, p.Z)
    p.sem("load", 6)
    p.sem("out")
    p.sem("halo", 2, 4)
    p.sem("tokt", 2)
    p.sem("dq", 2)
    p.sem("dkv", 2)
    p.sem("ret", 2, p.groups, blocks)
    return p


def kernel(p, tok_h, wq_h, wk_h, wv_h, cot_h, seg_h, gi_h, gq_ref, gk_ref, gv_ref, *refs):
    names = list(p.scratch)
    r = dict(zip(names, refs[: len(names)]))
    sm = dict(zip(p.sems, refs[len(names) :]))
    rows, lanes, blocks = p.rows, p.per * p.rows, p.reach + 1
    X, Y, Z, N, R = p.X, p.Y, p.Z, p.N, p.X
    z, me = lax.axis_index("dp"), lax.axis_index("ctx")
    core, chip = lax.rem(me, 2), me // 2
    cx, cy = chip // Y, lax.rem(chip, Y)
    peer = me + 1 - 2 * core
    nxt, prv = lax.rem(me + 2, N), lax.rem(me + N - 2, N)
    scale = HEAD**-0.5

    def along_x(o):
        return (lax.rem(cx + o, X) * Y + cy) * 2 + core

    def along_y(o):
        return (cx * Y + lax.rem(cy + o, Y)) * 2 + core

    def remote(src, dst, send, recv, ctx, dp=None):
        return pltpu.make_async_remote_copy(
            src_ref=src, dst_ref=dst, send_sem=send, recv_sem=recv,
            device_id=(z if dp is None else dp, ctx), device_id_type=MESH,
        )

    loads = {}
    for i, (name, src) in enumerate(
        (("tok", tok_h), ("wk", wk_h), ("wv", wv_h), ("wq", wq_h), ("cot", cot_h), ("seg", seg_h))
    ):
        loads[name] = pltpu.make_async_copy(src, r[name], sm["load"].at[i])
        loads[name].start()
    barrier = pltpu.get_barrier_semaphore()

    def greet(ctx, dp):
        pl.semaphore_signal(barrier, inc=1, device_id=(dp, ctx), device_id_type=MESH)

    def greet_z(o, c):
        greet(me, lax.rem(z + o, Z))
        return c

    lax.fori_loop(1, Z, greet_z, 0)
    for d in [peer, nxt, prv] + [along_x(o) for o in range(1, X)] + [along_y(o) for o in range(1, Y)]:
        greet(d, z)

    for name in ("tok", "wk", "wv"):
        loads[name].wait()
    for i, w in enumerate(("wk", "wv")):
        val = nn(r["tok"][...], r[w][...]).astype(BF)
        for g in range(p.groups):
            r["kvb"][0, i * p.groups + g] = val[:, g * HEAD : (g + 1) * HEAD]
    pl.semaphore_wait(barrier, 3 + (X - 1) + (Y - 1) + (Z - 1))

    kvb = r["kvb"]

    def halo(k, src, dst, to):
        return remote(kvb.at[src], kvb.at[dst], sm["halo"].at[0, k], sm["halo"].at[1, k], to)

    halo(0, 0, 2, nxt).start()

    @pl.when(core == 0)
    def _():
        halo(1, 0, 1, peer).start()

    loads["wq"].wait()
    step = 2 * HEAD
    for n in range(p.q_cols // step):
        val = nn(r["tok"][...], r["wq"][:, n * step : (n + 1) * step]).astype(BF)
        for j in range(2):
            g, h = divmod(2 * n + j, p.per)
            r["qst"][g, h * rows : (h + 1) * rows] = val[:, j * HEAD : (j + 1) * HEAD]
    loads["cot"].wait()
    for n in range(p.heads):
        g, h = divmod(n, p.per)
        r["dost"][g, h * rows : (h + 1) * rows] = r["cot"][:, n * HEAD : (n + 1) * HEAD]

    loads["seg"].wait()
    start = me * rows
    seg = r["seg"][...]
    q_seg = r["seg"][:, pl.ds(pl.multiple_of(start, rows), rows)]
    doc = jnp.zeros((1, rows), jnp.int32)
    for t in range(1, 4):
        below = jnp.sum((seg < t).astype(F32), axis=1, keepdims=True)
        doc = jnp.where(q_seg >= t, below.astype(jnp.int32), doc)
    row = lax.broadcasted_iota(jnp.int32, (rows, rows), 0)
    col = lax.broadcasted_iota(jnp.int32, (rows, rows), 1)
    for b in range(blocks):
        j = row + (start - b * rows)
        gap = col - row + b * rows
        ok = (j >= doc) & (gap >= 0) & (gap < WINDOW)
        r["bias"][b] = jnp.where(ok, 0.0, NEG)

    for n in range(p.width // HEAD):
        val = r["tok"][:, n * HEAD : (n + 1) * HEAD].astype(F32).T.astype(BF)
        for k in range(HEAD // p.own):
            ch, c = divmod(n * (HEAD // p.own) + k, 2)
            r["tokt"][c, ch * p.own : (ch + 1) * p.own] = val[k * p.own : (k + 1) * p.own]
    tokt_copy = remote(r["tokt"].at[1 - core], r["toktp"], sm["tokt"].at[0], sm["tokt"].at[1], peer)
    tokt_copy.start()

    r["m"][...] = jnp.full(r["m"].shape, -3e38, F32)

    def pass1(b):
        def body(g, c):
            kk, vv = kvb[b, g], kvb[b, p.groups + g]
            for h in range(p.per):
                cols = slice(h * rows, (h + 1) * rows)
                s = nt(kk, r["qst"][g, cols]) + r["bias"][b]
                r["s"][g, b, :, cols] = s
                r["m"][g, :, cols] = jnp.maximum(
                    r["m"][g, :, cols], jnp.max(s.reshape(rows // 8, 8, rows), axis=0)
                )
                r["dp"][g, b, :, cols] = nt(vv, r["dost"][g, cols])
            return c

        lax.fori_loop(0, p.groups, body, 0)

    pass1(0)
    halo(0, 0, 2, nxt).wait_recv()
    halo(2, 2, 4, nxt).start()

    @pl.when(core == 0)
    def _():
        halo(3, 2, 3, peer).start()

    @pl.when(core == 1)
    def _():
        halo(1, 2, 1, peer).start()

    pass1(2)
    halo(1, 0, 1, peer).wait_recv()
    pass1(1)
    halo(2, 2, 4, nxt).wait_recv()

    @pl.when(core == 1)
    def _():
        halo(3, 4, 3, peer).start()

    pass1(4)
    halo(3, 2, 3, peer).wait_recv()
    pass1(3)

    acc, stage, back = r["acc"], r["stage"], r["back"]
    first_core = (core == 0).astype(F32)
    second_core = (core == 1).astype(F32)

    def ret(g, d, to):
        return remote(stage.at[g, d], back.at[g, d], sm["ret"].at[0, g, d], sm["ret"].at[1, g, d], to)

    def pass2(g):
        m = jnp.max(r["m"][g], axis=0, keepdims=True)
        r["m"][g, 0:1] = m
        r["l"][...] = jnp.zeros(r["l"].shape, F32)
        r["de"][...] = jnp.zeros(r["de"].shape, F32)

        def expo(b, c):
            for h in range(p.per):
                cols = slice(h * rows, (h + 1) * rows)
                e = jnp.exp((r["s"][g, b, :, cols] - r["m"][g, 0:1, cols]) * scale)
                r["s"][g, b, :, cols] = e
                r["l"][:, cols] += jnp.sum(e.reshape(rows // 8, 8, rows), axis=0)
                de = e * r["dp"][g, b, :, cols]
                r["de"][:, cols] += jnp.sum(de.reshape(rows // 8, 8, rows), axis=0)
            return c

        lax.fori_loop(0, blocks, expo, 0)
        inv = 1.0 / jnp.sum(r["l"][...], axis=0, keepdims=True)
        delta = jnp.sum(r["de"][...], axis=0, keepdims=True) * inv
        r["l"][0:1] = inv
        r["de"][0:1] = delta
        r["dqt"][...] = jnp.zeros(r["dqt"].shape, F32)

        def grads(t, c):
            b = lax.rem(3 + 3 * t, blocks) if blocks == 5 else t
            kk = kvb[b, g]
            dv = jnp.zeros((rows, HEAD), F32)
            dk = jnp.zeros((rows, HEAD), F32)
            for h in range(p.per):
                cols = slice(h * rows, (h + 1) * rows)
                prob = r["s"][g, b, :, cols] * r["l"][0:1, cols]
                ds = (prob * (r["dp"][g, b, :, cols] - r["de"][0:1, cols]) * scale).astype(BF)
                dv = dv + nn(prob.astype(BF), r["dost"][g, cols])
                dk = dk + nn(ds, r["qst"][g, cols])
                r["dqt"][:, cols] += tn(kk, ds)
            acc[g, b, 0] = dk
            acc[g, b, 1] = dv
            stage[g, b, 0] = dk.astype(BF)
            stage[g, b, 1] = dv.astype(BF)
            return c

        lax.fori_loop(0, blocks, grads, 0)
        ret(g, 3, peer).start()
        ret(g, 1, peer).start()
        for h in range(p.per):
            n = g * p.per + h
            r["dq"][:, n * HEAD : (n + 1) * HEAD] = r["dqt"][:, h * rows : (h + 1) * rows].T.astype(BF)

    def ret4(g):
        ret(g, 3, peer).wait_recv()
        ret(g, 1, peer).wait_recv()
        stage[g, 4] = (acc[g, 4] + second_core * back[g, 3].astype(F32)).astype(BF)
        ret(g, 4, prv).start()

    def ret2(g):
        ret(g, 4, prv).wait_recv()
        t = acc[g, 2] + back[g, 4].astype(F32)
        t = t + first_core * back[g, 3].astype(F32) + second_core * back[g, 1].astype(F32)
        stage[g, 2] = t.astype(BF)
        ret(g, 2, prv).start()

    def ret0(g):
        ret(g, 2, prv).wait_recv()
        t = acc[g, 0] + back[g, 2].astype(F32) + first_core * back[g, 1].astype(F32)
        for i in range(2):
            r["dkv"][i, :, g * HEAD : (g + 1) * HEAD] = t[i].astype(BF)

    def made(i, grads):
        for j, (first, cols, x_first) in enumerate(p.parts[i]):
            mine, other = grads(j)
            one = r[f"one{i}{j}"]

            def block(a, c, mine=mine, other=other, one=one, x_first=x_first):
                at = pl.ds(pl.multiple_of(a * (Y * p.own), Y * p.own), Y * p.own)
                val = nn(r["tokt"][core, at], mine()) + nn(r["toktp"][at], other())
                val = val.astype(BF)
                if x_first:
                    one[a] = val
                else:
                    for k in range(Y):
                        one[k, pl.ds(pl.multiple_of(a * p.own, p.own), p.own)] = val[k * p.own : (k + 1) * p.own]
                return c

            lax.fori_loop(0, X, block, 0)

    def first_hop(i, j, o, x_first):
        at = lax.rem((cx if x_first else cy) + o, R)
        to = along_x(o) if x_first else along_y(o)
        s = sm[f"one{i}{j}"]
        return remote(r[f"one{i}{j}"].at[at], r[f"got{i}{j}"].at[o - 1], s.at[0, o], s.at[1, o], to)

    def second_hop(i, j, o, x_first):
        at = lax.rem((cy if x_first else cx) + o, R)
        to = along_y(o) if x_first else along_x(o)
        s = sm[f"two{i}{j}"]
        return remote(r[f"two{i}{j}"].at[at], r[f"gat{i}{j}"].at[o - 1], s.at[0, o], s.at[1, o], to)

    def start_first(i):
        for j, (_, _, x_first) in enumerate(p.parts[i]):
            for o in range(1, R):
                first_hop(i, j, o, x_first).start()

    def start_second(i):
        for j, (_, cols, x_first) in enumerate(p.parts[i]):
            t = r[f"one{i}{j}"][cx if x_first else cy].astype(F32)
            for o in range(1, R):
                first_hop(i, j, o, x_first).wait_recv()
                t = t + r[f"got{i}{j}"][o - 1].astype(F32)
            r[f"two{i}{j}"][...] = t.astype(BF).reshape(R, p.own, cols)
            for o in range(1, R):
                second_hop(i, j, o, x_first).start()

    def z_hop(i, o):
        to = lax.rem(z + o, Z)
        s = sm[f"zr{i}"]
        return remote(r[f"zs{i}"].at[to], r[f"zr{i}"].at[o], s.at[0, o], s.at[1, o], me, to)

    def z_gather(i, o):
        to = lax.rem(z + o, Z)
        s = sm[f"zo{i}"]
        return remote(r[f"zo{i}"].at[z], r[f"zo{i}"].at[z], s.at[0, o], s.at[1, o], me, to)

    def loop_z(f):
        def body(o, c):
            f(o)
            return c

        lax.fori_loop(1, Z, body, 0)

    def tiles_of(i):
        per_z = r[f"zs{i}"].shape[1] // 8
        ncb = sum(c for _, c, _ in p.parts[i]) // HEAD
        for t in range(per_z * Z):
            yield t // per_z, (t % per_z) * 8, (t // ncb) * 8, (t % ncb) * HEAD

    def start_z(i):
        pieces = []
        for j, (_, _, x_first) in enumerate(p.parts[i]):
            t = r[f"two{i}{j}"][cy if x_first else cx].astype(F32)
            for o in range(1, R):
                second_hop(i, j, o, x_first).wait_recv()
                t = t + r[f"gat{i}{j}"][o - 1].astype(F32)
            pieces.append(t)
        width = pieces[0].shape[1]
        for zi, zr, ro, co in tiles_of(i):
            part = pieces[co // width]
            co = co % width
            r[f"zs{i}"][zi, zr : zr + 8] = part[ro : ro + 8, co : co + HEAD]
        loop_z(lambda o: z_hop(i, o).start())

    def start_gather(i):
        loop_z(lambda o: z_hop(i, o).wait_recv())
        t = r[f"zs{i}"][z]
        for o in range(1, Z):
            t = t + r[f"zr{i}"][o]
        r[f"zo{i}"][z] = t * ((Z * N * rows) ** -0.5)
        loop_z(lambda o: z_gather(i, o).start())

    def finish(i):
        loop_z(lambda o: z_gather(i, o).wait_recv())
        for zi, zr, ro, co in tiles_of(i):
            val = r[f"zo{i}"][zi, zr : zr + 8]
            if i == 0:
                gq_ref[ro : ro + 8, co : co + HEAD] = val
            elif co < p.kv_cols:
                gk_ref[ro : ro + 8, co : co + HEAD] = val
            else:
                gv_ref[ro : ro + 8, co - p.kv_cols : co - p.kv_cols + HEAD] = val

    pass2(0)
    ret4(0)
    pass2(1)
    dq_copy = remote(r["dq"], r["dqp"], sm["dq"].at[0], sm["dq"].at[1], peer)
    dq_copy.start()
    ret4(1)
    ret2(0)
    tokt_copy.wait_recv()
    dq_copy.wait_recv()
    half = p.q_cols // 2
    made(0, lambda j: (lambda: r["dq"][:, j * half : (j + 1) * half], lambda: r["dqp"][:, j * half : (j + 1) * half]))
    start_first(0)
    ret2(1)

    def gi_q(n, c):
        at = pl.ds(pl.multiple_of(n * step, step), step)
        r["gi32"][:, at] = nt(r["dq"][...], r["wq"][at])
        return c

    lax.fori_loop(0, p.width // step, gi_q, 0)
    ret0(0)
    ret0(1)
    dkv_copy = remote(r["dkv"], r["dkvp"], sm["dkv"].at[0], sm["dkv"].at[1], peer)
    dkv_copy.start()

    def gi_kv(n, c):
        at = pl.ds(pl.multiple_of(n * step, step), step)
        val = r["gi32"][:, at] + nt(r["dkv"][0], r["wk"][at]) + nt(r["dkv"][1], r["wv"][at])
        r["gi"][:, at] = val.astype(BF)
        return c

    lax.fori_loop(0, p.width // step, gi_kv, 0)
    out_copy = pltpu.make_async_copy(r["gi"], gi_h, sm["out"])
    out_copy.start()
    dkv_copy.wait_recv()
    made(1, lambda j: (lambda: r["dkv"][j], lambda: r["dkvp"][j]))
    start_first(1)
    start_second(0)
    start_second(1)
    start_z(0)
    start_z(1)
    start_gather(0)
    start_gather(1)
    finish(0)
    finish(1)

    out_copy.wait()
    for k, (src, dst, to) in enumerate(((0, 2, nxt), (0, 1, peer), (2, 4, nxt), (2, 3, peer))):
        halo(k, src, dst, to).wait_send()
    tokt_copy.wait_send()
    dq_copy.wait_send()
    dkv_copy.wait_send()
    for g in range(p.groups):
        for d, to in ((3, peer), (1, peer), (4, prv), (2, prv)):
            ret(g, d, to).wait_send()
    for i in range(2):
        for j, (_, _, x_first) in enumerate(p.parts[i]):
            for o in range(1, R):
                first_hop(i, j, o, x_first).wait_send()
                second_hop(i, j, o, x_first).wait_send()
        loop_z(lambda o: z_hop(i, o).wait_send())
        loop_z(lambda o: z_gather(i, o).wait_send())


def body(sizes, tokens, w_query, key_weight, value_weight, cotangent, segment_ids):
    rows, width = tokens.shape[1:]
    q_cols, kv_cols = w_query.shape[1], key_weight.shape[1]
    p = build_plan(sizes, rows, width, q_cols, kv_cols, segment_ids.shape[1])
    anyspace = pl.BlockSpec(memory_space=pl.ANY)
    vmem = pl.BlockSpec(memory_space=pltpu.VMEM)
    out = pl.pallas_call(
        functools.partial(kernel, p),
        out_shape=(
            jax.ShapeDtypeStruct((rows, width), BF),
            jax.ShapeDtypeStruct((p.own, q_cols), F32),
            jax.ShapeDtypeStruct((p.own, kv_cols), F32),
            jax.ShapeDtypeStruct((p.own, kv_cols), F32),
        ),
        in_specs=[anyspace] * 6,
        out_specs=(anyspace, vmem, vmem, vmem),
        scratch_shapes=list(p.scratch.values()) + list(p.sems.values()),
        compiler_params=pltpu.CompilerParams(
            collective_id=0, has_side_effects=True, vmem_limit_bytes=60 * 1024 * 1024
        ),
        name="step",
    )(tokens[0], w_query, key_weight, value_weight, cotangent[0], segment_ids)
    return out[0][None], out[1], out[2], out[3]


def solution(mesh):
    sizes = dict(mesh.shape)
    placed = (P("dp", "ctx", None), P(), P(), P(), P("dp", "ctx", None), P("dp", None))
    return jax.shard_map(
        functools.partial(body, sizes),
        mesh=mesh,
        in_specs=placed,
        out_specs=(P("dp", "ctx", None), P("ctx", None), P("ctx", None), P("ctx", None)),
        check_vma=False,
    )
```

```python
import functools
import math

import jax
import jax.numpy as jnp
from jax import lax
from jax.experimental import pallas as pl
from jax.experimental.pallas import tpu as pltpu
from jax.sharding import PartitionSpec as P

HEAD = 128
WINDOW = 1024
NEG = -1e30
VMEM_LIMIT = 54 * 1024 * 1024
BF = jnp.bfloat16
F32 = jnp.float32
MESH = pl.DeviceIdType.MESH
TRACE = False


def mark(name, f, *a):
    if not TRACE:
        return f(*a)
    with jax.named_scope(name):
        return f(*a)


def nn(a, b):
    return lax.dot_general(a, b, (((1,), (0,)), ((), ())), preferred_element_type=F32)


def nt(a, b):
    return lax.dot_general(a, b, (((1,), (1,)), ((), ())), preferred_element_type=F32)


def tn(a, b):
    return lax.dot_general(a, b, (((0,), (0,)), ((), ())), preferred_element_type=F32)


class Plan:
    def __init__(self, sizes, rows, width, q_cols, kv_cols, length):
        self.Z, self.N = sizes["dp"], sizes["ctx"]
        self.X = self.Y = math.isqrt(self.N // 2)
        self.rows, self.width, self.q_cols, self.kv_cols = rows, width, q_cols, kv_cols
        self.length = length
        self.heads = q_cols // HEAD
        self.groups = kv_cols // HEAD
        self.per = self.heads // self.groups
        self.reach = WINDOW // rows
        self.chips = self.N // 2
        self.own = width // self.N
        half = q_cols // 2
        self.q_pieces = ((0, half, True), (half, half, True))
        self.kv_pieces = ((q_cols, kv_cols, True), (q_cols + kv_cols, kv_cols, False))
        self.parts = (self.q_pieces, self.kv_pieces)
        self.scratch = {}
        self.sems = {}

    def cut(self, phase, part):
        if phase == "one":
            return 0 if part == 0 else self.X * self.own // 2
        return self.own // 2

    def buf(self, name, shape, dtype):
        self.scratch[name] = pltpu.VMEM(shape, dtype)

    def sem(self, name, *shape):
        self.sems[name] = pltpu.SemaphoreType.DMA(shape)


def build_plan(sizes, rows, width, q_cols, kv_cols, length):
    p = Plan(sizes, rows, width, q_cols, kv_cols, length)
    lanes = p.per * rows
    blocks = p.reach + 1
    p.buf("tok", (rows, width), BF)
    p.buf("wq", (width, q_cols), BF)
    p.buf("wk", (width, kv_cols), BF)
    p.buf("wv", (width, kv_cols), BF)
    p.buf("cot", (rows, q_cols), BF)
    p.buf("seg", (1, length), jnp.int32)
    p.buf("kvb", (blocks, 2 * p.groups, rows, HEAD), BF)
    p.buf("qst", (p.groups, lanes, HEAD), BF)
    p.buf("dost", (p.groups, lanes, HEAD), BF)
    p.buf("bias", (blocks, rows, rows), F32)
    p.buf("s", (p.groups, blocks, rows, lanes), F32)
    p.buf("dp", (p.groups, blocks, rows, lanes), F32)
    p.buf("relay", (2, rows, HEAD), BF)
    p.buf("m", (p.groups, 8, lanes), F32)
    p.buf("top", (p.groups, 8, lanes), F32)
    p.buf("l", (p.groups, 8, lanes), F32)
    p.buf("de", (p.groups, 8, lanes), F32)
    p.buf("fac", (p.groups, 8, lanes), F32)
    p.buf("acc", (p.groups, blocks, 2, rows, HEAD), F32)
    p.buf("dqt", (p.groups, HEAD, lanes), F32)
    p.buf("relay_back", (p.groups, rows, HEAD), BF)
    p.buf("far", (p.groups, rows, HEAD), BF)
    p.buf("stage", (p.groups, blocks, 2, rows, HEAD), BF)
    p.buf("back", (p.groups, blocks, 2, rows, HEAD), BF)
    p.buf("tokt", (2, width // 2, rows), BF)
    p.buf("toktp", (width // 2, rows), BF)
    p.buf("dq", (rows, q_cols), BF)
    p.buf("dqp", (rows, q_cols), BF)
    p.buf("dkv", (p.groups, 2, rows, HEAD), BF)
    p.buf("dkvp", (p.groups, 2, rows, HEAD), BF)
    p.buf("gi32", (rows, width), F32)
    own, R = p.own, p.X
    for i, part in enumerate(p.parts):
        for j, (first, cols, x_first) in enumerate(part):
            for k, n in (("one", R * own), ("two", own)):
                cut = p.cut(k, i)
                name = f"{k}{i}{j}"
                p.buf(name, (R, n, cols), BF)
                if cut:
                    p.buf(name + "down", (cut, cols), BF)
                p.buf(name + "up", (n - cut, cols), BF)
                p.buf(name + "left", (n, cols), BF)
                p.buf(name + "right", (n, cols), BF)
                p.sem(name, 2, 6)
        tiles = own // 8 * sum(c for _, c, _ in part) // HEAD
        p.buf(f"zs{i}", (p.Z, tiles // p.Z * 8, HEAD), F32)
        p.buf(f"zr{i}", (p.Z, tiles // p.Z * 8, HEAD), F32)
        p.buf(f"zo{i}", (p.Z, tiles // p.Z * 8, HEAD), F32)
        p.sem(f"zr{i}", 2, p.Z)
        p.sem(f"zo{i}", 2, p.Z)
    p.sem("load", 6)
    p.sems["z_in"] = pltpu.SemaphoreType.REGULAR((2,))
    p.sem("ha", 2, 2 * p.groups)
    p.sem("hb", 2)
    p.sem("hc", 2, p.groups)
    p.sem("hd", 2)
    p.sem("he", 2)
    p.sem("hf", 2)
    p.sem("tokt", 2)
    p.sem("dq", 2)
    p.sem("dkv", 2, p.groups)
    p.sem("far", 2, p.groups)
    p.sem("relay_back", 2, p.groups)
    p.sem("ret", 2, p.groups, blocks)
    return p


def kernel(p, tok_h, wq_h, wk_h, wv_h, cot_h, seg_h, gi_ref, gq_ref, gk_ref, gv_ref, *refs):
    names = list(p.scratch)
    r = dict(zip(names, refs[: len(names)]))
    sm = dict(zip(p.sems, refs[len(names) :]))
    rows, lanes, blocks = p.rows, p.per * p.rows, p.reach + 1
    X, Y, Z, N, R = p.X, p.Y, p.Z, p.N, p.X
    z, me = lax.axis_index("dp"), lax.axis_index("ctx")
    core, chip = lax.rem(me, 2), me // 2
    cx, cy = chip // Y, lax.rem(chip, Y)
    peer = me + 1 - 2 * core
    nxt, prv = lax.rem(me + 2, N), lax.rem(me + N - 2, N)
    far_to = lax.rem(cx * Y + lax.rem(cy + 1, Y) + 2, p.chips) * 2 + core
    back2 = lax.rem(chip + p.chips - 2, p.chips)
    far_from = (back2 // Y * Y + lax.rem(lax.rem(back2, Y) + Y - 1, Y)) * 2 + core
    scale = HEAD**-0.5

    def along_x(o):
        return (lax.rem(cx + o, X) * Y + cy) * 2 + core

    def along_y(o):
        return (cx * Y + lax.rem(cy + o, Y)) * 2 + core

    def remote(src, dst, send, recv, ctx, dp=None):
        return pltpu.make_async_remote_copy(
            src_ref=src, dst_ref=dst, send_sem=send, recv_sem=recv,
            device_id=(z if dp is None else dp, ctx), device_id_type=MESH,
        )

    loads = {}
    for i, (name, src) in enumerate(
        (("tok", tok_h), ("wk", wk_h), ("wv", wv_h), ("wq", wq_h), ("cot", cot_h), ("seg", seg_h))
    ):
        loads[name] = pltpu.make_async_copy(src, r[name], sm["load"].at[i])
        loads[name].start()
    barrier = pltpu.get_barrier_semaphore()

    def greet(ctx, dp):
        pl.semaphore_signal(barrier, inc=1, device_id=(dp, ctx), device_id_type=MESH)

    near_z = min(3, Z)
    for o in range(1, near_z):
        greet(me, lax.rem(z + o, Z))
        greet(me, lax.rem(z + Z - o, Z))
    ring = [along_x(o) for o in (1, X - 1)] + [along_y(o) for o in (1, Y - 1)]
    for d in [peer, nxt, prv, far_to, far_from] + ring:
        greet(d, z)

    def z_round(k, distance):
        if Z <= distance:
            return
        for to in (lax.rem(z + distance, Z), lax.rem(z + Z - distance, Z)):
            pl.semaphore_signal(sm["z_in"].at[k], inc=1, device_id=(to, me), device_id_type=MESH)

    def z_joined(k, distance):
        if Z > distance:
            pl.semaphore_wait(sm["z_in"].at[k], 2)

    mark("w_tok", lambda: [loads[name].wait() for name in ("tok", "wk", "wv")])
    for i, w in enumerate(("wk", "wv")):
        val = nn(r["tok"][...], r[w][...]).astype(BF)
        for g in range(p.groups):
            r["kvb"][0, i * p.groups + g] = val[:, g * HEAD : (g + 1) * HEAD]
    mark('w_bar', pl.semaphore_wait, barrier, 9 + 2 * (near_z - 1))
    z_round(0, 2)

    kvb = r["kvb"]

    G, both = p.groups, 2 * p.groups
    up = along_y(Y - 1)

    def pair(name, *at):
        x = sm[name]
        return x.at[(0, *at)], x.at[(1, *at)]

    def h_next(u):
        return remote(kvb.at[0, u], kvb.at[2, u], *pair("ha", u), nxt)

    def h_one(src):
        return remote(kvb.at[src], kvb.at[1], *pair("hb"), peer)

    def h_four(u):
        return remote(kvb.at[2, u], kvb.at[4, u], *pair("hc", u), nxt)

    def h_three(src):
        return remote(kvb.at[src], kvb.at[3], *pair("hd"), peer)

    far_one = remote(kvb.at[0, pl.ds(G, G)], r["relay"], *pair("he"), up)
    far_two = remote(r["relay"], kvb.at[4, pl.ds(G, G)], *pair("hf"), far_to)
    h_next(0).start()
    far_one.start()
    for u in range(1, both):
        h_next(u).start()

    @pl.when(core == 0)
    def _():
        h_one(0).start()

    mark("w_wq", loads["wq"].wait)
    step = 2 * HEAD
    for n in range(p.q_cols // step):
        val = nn(r["tok"][...], r["wq"][:, n * step : (n + 1) * step]).astype(BF)
        for j in range(2):
            g, h = divmod(2 * n + j, p.per)
            r["qst"][g, h * rows : (h + 1) * rows] = val[:, j * HEAD : (j + 1) * HEAD]
    mark("w_cot", loads["cot"].wait)
    for n in range(p.heads):
        g, h = divmod(n, p.per)
        r["dost"][g, h * rows : (h + 1) * rows] = r["cot"][:, n * HEAD : (n + 1) * HEAD]

    mark("w_seg", loads["seg"].wait)
    start = me * rows
    seg = r["seg"][...]
    q_seg = r["seg"][:, pl.ds(pl.multiple_of(start, rows), rows)]
    doc = jnp.zeros((1, rows), jnp.int32)
    for t in range(1, 4):
        below = jnp.sum((seg < t).astype(F32), axis=1, keepdims=True)
        doc = jnp.where(q_seg >= t, below.astype(jnp.int32), doc)
    row = lax.broadcasted_iota(jnp.int32, (rows, rows), 0)
    col = lax.broadcasted_iota(jnp.int32, (rows, rows), 1)
    for b in range(blocks):
        j = row + (start - b * rows)
        gap = col - row + b * rows
        ok = (j >= doc) & (gap >= 0) & (gap < WINDOW)
        r["bias"][b] = jnp.where(ok, 0.0, NEG)

    for n in range(p.width // HEAD):
        val = r["tok"][:, n * HEAD : (n + 1) * HEAD].astype(F32).T.astype(BF)
        for k in range(HEAD // p.own):
            ch, c = divmod(n * (HEAD // p.own) + k, 2)
            r["tokt"][c, ch * p.own : (ch + 1) * p.own] = val[k * p.own : (k + 1) * p.own]
    tokt_copy = remote(r["tokt"].at[1 - core], r["toktp"], sm["tokt"].at[0], sm["tokt"].at[1], peer)
    tokt_copy.start()

    r["m"][...] = jnp.full(r["m"].shape, -3e38, F32)

    def pass1(b):
        def body(g, c):
            kk, vv = kvb[b, g], kvb[b, p.groups + g]
            for h in range(p.per):
                cols = slice(h * rows, (h + 1) * rows)
                s = nt(kk, r["qst"][g, cols]) + r["bias"][b]
                r["s"][g, b, :, cols] = s
                r["m"][g, :, cols] = jnp.maximum(
                    r["m"][g, :, cols], jnp.max(s.reshape(rows // 8, 8, rows), axis=0)
                )
                r["dp"][g, b, :, cols] = nt(vv, r["dost"][g, cols])
            return c

        lax.fori_loop(0, p.groups, body, 0)

    mark("pass1_0", pass1, 0)
    for u in range(G):
        mark("w_next", h_next(u).wait_recv)
        h_four(u).start()
    mark("w_far", far_one.wait_recv)
    far_two.start()
    for u in range(G, both):
        mark("w_next2", h_next(u).wait_recv)

    @pl.when(core == 0)
    def _():
        h_three(2).start()

    @pl.when(core == 1)
    def _():
        h_one(2).start()

    mark("pass1_2", pass1, 2)
    mark("w_one", h_one(0).wait_recv)
    mark("pass1_1", pass1, 1)

    r["l"][...] = jnp.zeros(r["l"].shape, F32)
    r["de"][...] = jnp.zeros(r["de"].shape, F32)

    def expo(g, b):
        for h in range(p.per):
            cols = slice(h * rows, (h + 1) * rows)
            e = jnp.exp((r["s"][g, b, :, cols] - r["top"][g, 0:1, cols]) * scale)
            r["s"][g, b, :, cols] = e
            r["l"][g, :, cols] += jnp.sum(e.reshape(rows // 8, 8, rows), axis=0)
            de = e * r["dp"][g, b, :, cols]
            r["de"][g, :, cols] += jnp.sum(de.reshape(rows // 8, 8, rows), axis=0)

    def early(g, c):
        r["top"][g] = jnp.broadcast_to(jnp.max(r["m"][g], axis=0, keepdims=True), (8, lanes))

        def one(b, c2):
            expo(g, b)
            return c2

        return lax.fori_loop(0, 3, one, c)

    def late(g, c):
        top = jnp.broadcast_to(jnp.max(r["m"][g], axis=0, keepdims=True), (8, lanes))
        down = jnp.exp((r["top"][g] - top) * scale)
        r["top"][g] = top
        r["fac"][g] = down
        r["l"][g] *= down
        r["de"][g] *= down

        def one(b, c2):
            expo(g, b)
            return c2

        lax.fori_loop(3, blocks, one, c)
        inv = 1.0 / jnp.sum(r["l"][g], axis=0, keepdims=True)
        delta = jnp.sum(r["de"][g], axis=0, keepdims=True) * inv
        r["l"][g] = jnp.broadcast_to(inv, (8, lanes))
        r["de"][g] = jnp.broadcast_to(delta, (8, lanes))
        return c

    z_joined(0, 2)
    z_round(1, 4)
    mark("early", lax.fori_loop, 0, G, early, 0)
    for u in range(G):
        mark("w_four", h_four(u).wait_recv)
    mark("w_far2", far_two.wait_recv)

    @pl.when(core == 1)
    def _():
        h_three(4).start()

    mark("pass1_4", pass1, 4)
    mark("w_three", h_three(2).wait_recv)
    mark("pass1_3", pass1, 3)
    mark("late", lax.fori_loop, 0, G, late, 0)

    acc, stage, back = r["acc"], r["stage"], r["back"]
    first_core = (core == 0).astype(F32)
    second_core = (core == 1).astype(F32)
    r["dqt"][...] = jnp.zeros(r["dqt"].shape, F32)

    def grads(b):
        def body(g, c):
            kk = kvb[b, g]
            dv = jnp.zeros((rows, HEAD), F32)
            dk = jnp.zeros((rows, HEAD), F32)
            for h in range(p.per):
                cols = slice(h * rows, (h + 1) * rows)
                inv = r["l"][g, 0:1, cols]
                if b < 3:
                    inv = inv * r["fac"][g, 0:1, cols]
                prob = r["s"][g, b, :, cols] * inv
                ds = (prob * (r["dp"][g, b, :, cols] - r["de"][g, 0:1, cols]) * scale).astype(BF)
                dv = dv + nn(prob.astype(BF), r["dost"][g, cols])
                dk = dk + nn(ds, r["qst"][g, cols])
                r["dqt"][g, :, cols] += tn(kk, ds)
            acc[g, b, 0] = dk
            acc[g, b, 1] = dv
            if b in (1, 3, 4):
                stage[g, b, 0] = dk.astype(BF)
                stage[g, b, 1] = dv.astype(BF)
            return c

        lax.fori_loop(0, G, body, 0)

    def ret(g, d, to):
        return remote(stage.at[g, d], back.at[g, d], *pair("ret", g, d), to)

    def ret_four(g):
        return remote(stage.at[g, 4, 0], back.at[g, 4, 0], *pair("ret", g, 4), prv)

    def far_send(g):
        return remote(stage.at[g, 4, 1], r["relay_back"].at[g], *pair("relay_back", g), far_from)

    def far_last(g):
        return remote(r["relay_back"].at[g], r["far"].at[g], *pair("far", g), along_y(1))

    def to_peer(d):
        for g in range(G):
            ret(g, d, peer).start()

    def ret4(g):
        @pl.when(core == 1)
        def _():
            ret(g, 3, peer).wait_recv()
            stage[g, 4] = (acc[g, 4] + back[g, 3].astype(F32)).astype(BF)

        ret_four(g).start()
        far_send(g).start()

    def forward_far(g):
        far_send(g).wait_recv()
        far_last(g).start()

    def ret2(g):
        @pl.when(core == 0)
        def _():
            ret(g, 3, peer).wait_recv()

        ret(g, 1, peer).wait_recv()
        ret_four(g).wait_recv()
        t = acc[g, 2] + first_core * back[g, 3].astype(F32) + second_core * back[g, 1].astype(F32)
        stage[g, 2, 0] = (t[0] + back[g, 4, 0].astype(F32)).astype(BF)
        stage[g, 2, 1] = t[1].astype(BF)
        ret(g, 2, prv).start()

    def dkv_copy(g):
        return remote(r["dkv"].at[g], r["dkvp"].at[g], *pair("dkv", g), peer)

    def ret0(g):
        ret(g, 2, prv).wait_recv()
        far_last(g).wait_recv()
        t = acc[g, 0] + back[g, 2].astype(F32) + first_core * back[g, 1].astype(F32)
        r["dkv"][g, 0] = t[0].astype(BF)
        r["dkv"][g, 1] = (t[1] + r["far"][g].astype(F32)).astype(BF)
        dkv_copy(g).start()

    def made(one, x_first, at, mine, other):
        val = (nn(r["tokt"][core], mine) + nn(r["toktp"][...], other)).astype(BF)
        if x_first:
            one[:, :, at] = val.reshape(X, Y * p.own, val.shape[1])
        else:
            for a in range(X):
                for k in range(Y):
                    ro = (a * Y + k) * p.own
                    one[k, a * p.own : (a + 1) * p.own, at] = val[ro : ro + p.own]

    def made_q(j):
        first, cols, x_first = p.parts[0][j]

        def body(n, c):
            to = pl.ds(pl.multiple_of(n * step, step), step)
            at = pl.ds(pl.multiple_of(first + n * step, step), step)
            made(r[f"one0{j}"], x_first, to, r["dq"][:, at], r["dqp"][:, at])
            return c

        lax.fori_loop(0, cols // step, body, 0)

    def made_kv(j):
        def wide(name):
            return jnp.concatenate([r[name][g, j] for g in range(G)], axis=1)

        made(r[f"one1{j}"], p.parts[1][j][2], slice(0, p.kv_cols), wide("dkv"), wide("dkvp"))

    class Ring:
        def __init__(self, k, i, j):
            x_first = p.parts[i][j][2]
            on_x = x_first == (k == "one")
            self.name, self.cut = f"{k}{i}{j}", p.cut(k, i)
            self.at, along = (cx, along_x) if on_x else (cy, along_y)
            self.next, self.prev = along(1), along(R - 1)
            self.n = r[self.name].shape[1]

        def chunk(self, o):
            return r[self.name].at[lax.rem(self.at + o, R)]

        def copy(self, k, src, dst, to):
            return remote(src, dst, *pair(self.name, k), to)

        def two_up(self):
            return self.copy(0, self.chunk(2).at[self.cut :], r[self.name + "up"], self.next)

        def two_down(self):
            return self.copy(1, self.chunk(2).at[: self.cut], r[self.name + "down"], self.prev)

        def up(self, rows, k):
            return self.copy(k, self.chunk(1).at[rows], r[self.name + "left"].at[rows], self.next)

        def down(self, rows, k):
            return self.copy(k, self.chunk(R - 1).at[rows], r[self.name + "right"].at[rows], self.prev)

        def start_up(self):
            self.two_up().start()
            if self.cut:
                self.up(slice(0, self.cut), 2).start()

        def start_down(self):
            if self.cut:
                self.two_down().start()
            self.down(slice(self.cut, self.n), 3).start()

        def add(self, o, rows, name):
            k = lax.rem(self.at + o, R)
            val = r[self.name][k, rows].astype(F32) + r[self.name + name][...].astype(F32)
            r[self.name][k, rows] = val.astype(BF)

        def pass_up(self):
            self.two_up().wait_recv()
            self.add(1, slice(self.cut, self.n), "up")
            self.up(slice(self.cut, self.n), 4).start()

        def pass_down(self):
            if self.cut:
                self.two_down().wait_recv()
                self.add(R - 1, slice(0, self.cut), "down")
                self.down(slice(0, self.cut), 5).start()

        def copies(self, whole=True):
            if whole:
                yield self.two_up()
            yield self.down(slice(self.cut, self.n), 3)
            yield self.up(slice(self.cut, self.n), 4)
            if self.cut:
                if whole:
                    yield self.two_down()
                yield self.up(slice(0, self.cut), 2)
                yield self.down(slice(0, self.cut), 5)

        def total(self):
            for copy in self.copies(whole=False):
                copy.wait_recv()
            t = r[self.name][self.at].astype(F32)
            return t + r[self.name + "left"][...].astype(F32) + r[self.name + "right"][...].astype(F32)

    one = [[Ring("one", i, j) for j in range(2)] for i in range(2)]
    two = [[Ring("two", i, j) for j in range(2)] for i in range(2)]

    def start_second(i):
        for j in range(2):
            t = one[i][j].total().astype(BF)
            r[f"two{i}{j}"][...] = t.reshape(R, p.own, t.shape[1])
            two[i][j].start_up()
            two[i][j].start_down()

    def pass_second(i):
        for j in range(2):
            two[i][j].pass_up()
            two[i][j].pass_down()

    def z_hop(i, o):
        to = lax.rem(z + o, Z)
        s = sm[f"zr{i}"]
        return remote(r[f"zs{i}"].at[to], r[f"zr{i}"].at[o], s.at[0, o], s.at[1, o], me, to)

    def z_gather(i, o):
        to = lax.rem(z + o, Z)
        s = sm[f"zo{i}"]
        return remote(r[f"zo{i}"].at[z], r[f"zo{i}"].at[z], s.at[0, o], s.at[1, o], me, to)

    def loop_z(f):
        def body(o, c):
            f(o)
            return c

        lax.fori_loop(1, Z, body, 0)

    def tiles_of(i):
        per_z = r[f"zs{i}"].shape[1] // 8
        ncb = sum(c for _, c, _ in p.parts[i]) // HEAD
        for t in range(per_z * Z):
            yield t // per_z, (t % per_z) * 8, (t // ncb) * 8, (t % ncb) * HEAD

    def start_z(i):
        pieces = [two[i][j].total() for j in range(2)]
        width = pieces[0].shape[1]
        for zi, zr, ro, co in tiles_of(i):
            part = pieces[co // width]
            co = co % width
            r[f"zs{i}"][zi, zr : zr + 8] = part[ro : ro + 8, co : co + HEAD]
        loop_z(lambda o: z_hop(i, o).start())

    def start_gather(i):
        loop_z(lambda o: z_hop(i, o).wait_recv())
        t = r[f"zs{i}"][z]
        for o in range(1, Z):
            t = t + r[f"zr{i}"][o]
        r[f"zo{i}"][z] = t * ((Z * N * rows) ** -0.5)
        loop_z(lambda o: z_gather(i, o).start())

    def finish(i):
        loop_z(lambda o: z_gather(i, o).wait_recv())
        for zi, zr, ro, co in tiles_of(i):
            val = r[f"zo{i}"][zi, zr : zr + 8]
            if i == 0:
                gq_ref[ro : ro + 8, co : co + HEAD] = val
            elif co < p.kv_cols:
                gk_ref[ro : ro + 8, co : co + HEAD] = val
            else:
                gv_ref[ro : ro + 8, co - p.kv_cols : co - p.kv_cols + HEAD] = val

    z_joined(1, 4)
    mark("grads3", grads, 3)
    to_peer(3)
    mark("grads1", grads, 1)
    to_peer(1)
    mark("grads4", grads, 4)
    mark("ret4", lambda: [ret4(g) for g in range(G)])
    mark("grads2", grads, 2)
    mark("grads0", grads, 0)

    def dq_rows():
        for n in range(p.heads):
            g, h = divmod(n, p.per)
            r["dq"][:, n * HEAD : (n + 1) * HEAD] = r["dqt"][g, :, h * rows : (h + 1) * rows].T.astype(BF)

    mark("dq_rows", dq_rows)
    dq_copy = remote(r["dq"], r["dqp"], *pair("dq"), peer)
    dq_copy.start()
    mark("w_dq", lambda: (tokt_copy.wait_recv(), dq_copy.wait_recv()))
    mark("made_q", made_q, 0)
    one[0][0].start_up()
    mark("fwd_far", lambda: [forward_far(g) for g in range(G)])
    mark("ret2_0", ret2, 0)
    mark("made_q", made_q, 1)
    one[0][1].start_up()
    mark("ret2_1", ret2, 1)

    def gi_q(n, c):
        at = pl.ds(pl.multiple_of(n * step, step), step)
        r["gi32"][:, at] = nt(r["dq"][...], r["wq"][at])
        return c

    mark("gi_q", lax.fori_loop, 0, p.width // step, gi_q, 0)
    mark("ret0_0", ret0, 0)
    mark("pass_q", one[0][0].pass_up)
    one[0][0].start_down()
    mark("ret0_1", ret0, 1)
    mark("pass_q", one[0][1].pass_up)
    one[0][1].start_down()
    mark("w_dkv", lambda: [dkv_copy(g).wait_recv() for g in range(G)])
    for j in range(2):
        mark("made_kv", made_kv, j)
        one[1][j].start_up()
        one[1][j].start_down()

    def gi_kv(n, c):
        at = pl.ds(pl.multiple_of(n * step, step), step)
        val = r["gi32"][:, at]
        for i, w in enumerate(("wk", "wv")):
            for g in range(G):
                val = val + nt(r["dkv"][g, i], r[w][at, g * HEAD : (g + 1) * HEAD])
        gi_ref[:, at] = val.astype(BF)
        return c

    mark("gi_kv", lax.fori_loop, 0, p.width // step, gi_kv, 0)
    mark("pass_kv", lambda: [f() for j in range(2) for f in (one[1][j].pass_up, one[1][j].pass_down)])
    mark("second_0", start_second, 0)
    mark("second_1", start_second, 1)
    mark("pass2_0", pass_second, 0)
    mark("pass2_1", pass_second, 1)
    mark("z_0", start_z, 0)
    mark("z_1", start_z, 1)
    mark("gather_0", start_gather, 0)
    mark("gather_1", start_gather, 1)
    mark("finish_0", finish, 0)
    mark("finish_1", finish, 1)

    for u in range(both):
        h_next(u).wait_send()
    for u in range(G):
        h_four(u).wait_send()
    for copy in (h_one(0), h_three(2), far_one, far_two, tokt_copy, dq_copy):
        copy.wait_send()
    for g in range(G):
        for copy in (ret(g, 3, peer), ret(g, 1, peer), ret(g, 2, prv), ret_four(g), far_send(g), far_last(g), dkv_copy(g)):
            copy.wait_send()
    for i in range(2):
        for ring_sum in one[i] + two[i]:
            for copy in ring_sum.copies():
                copy.wait_send()
        loop_z(lambda o: z_hop(i, o).wait_send())
        loop_z(lambda o: z_gather(i, o).wait_send())


def emit(*refs):
    n = (len(refs) - 1) // 2
    copies = [pltpu.make_async_copy(refs[i], refs[n + i], refs[-1].at[i]) for i in range(n)]
    for c in copies:
        c.start()
    for c in copies:
        c.wait()


def body(sizes, tokens, w_query, key_weight, value_weight, cotangent, segment_ids):
    rows, width = tokens.shape[1:]
    q_cols, kv_cols = w_query.shape[1], key_weight.shape[1]
    p = build_plan(sizes, rows, width, q_cols, kv_cols, segment_ids.shape[1])
    anyspace = pl.BlockSpec(memory_space=pl.ANY)
    vmem = pl.BlockSpec(memory_space=pltpu.VMEM)
    shapes = (
        jax.ShapeDtypeStruct((rows, width), BF),
        jax.ShapeDtypeStruct((p.own, q_cols), F32),
        jax.ShapeDtypeStruct((p.own, kv_cols), F32),
        jax.ShapeDtypeStruct((p.own, kv_cols), F32),
    )
    out = pl.pallas_call(
        functools.partial(kernel, p),
        out_shape=shapes,
        in_specs=[anyspace] * 6,
        out_specs=(vmem,) * 4,
        scratch_shapes=list(p.scratch.values()) + list(p.sems.values()),
        compiler_params=pltpu.CompilerParams(
            collective_id=0, has_side_effects=True, vmem_limit_bytes=VMEM_LIMIT
        ),
        name="step",
    )(tokens[0], w_query, key_weight, value_weight, cotangent[0], segment_ids)
    out = pl.pallas_call(
        emit,
        out_shape=shapes,
        in_specs=[vmem] * 4,
        out_specs=(anyspace,) * 4,
        scratch_shapes=[pltpu.SemaphoreType.DMA((4,))],
        name="emit",
    )(*out)
    return out[0][None], out[1], out[2], out[3]


def solution(mesh):
    sizes = dict(mesh.shape)
    placed = (P("dp", "ctx", None), P(), P(), P(), P("dp", "ctx", None), P("dp", None))
    return jax.shard_map(
        functools.partial(body, sizes),
        mesh=mesh,
        in_specs=placed,
        out_specs=(P("dp", "ctx", None), P("ctx", None), P("ctx", None), P("ctx", None)),
        check_vma=False,
    )
```

```python
import functools
import math

import jax
import jax.numpy as jnp
from jax import lax
from jax.experimental import pallas as pl
from jax.experimental.pallas import tpu as pltpu
from jax.sharding import PartitionSpec as P

HEAD = 128
WINDOW = 1024
NEG = -1e30
VMEM_LIMIT = 54 * 1024 * 1024
BF = jnp.bfloat16
F32 = jnp.float32
MESH = pl.DeviceIdType.MESH
TRACE = False


def mark(name, f, *a):
    if not TRACE:
        return f(*a)
    with jax.named_scope(name):
        return f(*a)


def nn(a, b):
    return lax.dot_general(a, b, (((1,), (0,)), ((), ())), preferred_element_type=F32)


def nt(a, b):
    return lax.dot_general(a, b, (((1,), (1,)), ((), ())), preferred_element_type=F32)


def tn(a, b):
    return lax.dot_general(a, b, (((0,), (0,)), ((), ())), preferred_element_type=F32)


class Plan:
    def __init__(self, sizes, rows, width, q_cols, kv_cols, length):
        self.Z, self.N = sizes["dp"], sizes["ctx"]
        self.X = self.Y = math.isqrt(self.N // 2)
        self.rows, self.width, self.q_cols, self.kv_cols = rows, width, q_cols, kv_cols
        self.length = length
        self.heads = q_cols // HEAD
        self.groups = kv_cols // HEAD
        self.per = self.heads // self.groups
        self.reach = WINDOW // rows
        self.chips = self.N // 2
        self.own = width // self.N
        half = q_cols // 2
        self.q_pieces = ((0, half, True), (half, half, True))
        self.kv_pieces = ((q_cols, kv_cols, True), (q_cols + kv_cols, kv_cols, False))
        self.parts = (self.q_pieces, self.kv_pieces)
        self.scratch = {}
        self.sems = {}

    def buf(self, name, shape, dtype):
        self.scratch[name] = pltpu.VMEM(shape, dtype)

    def sem(self, name, *shape):
        self.sems[name] = pltpu.SemaphoreType.DMA(shape)


def build_plan(sizes, rows, width, q_cols, kv_cols, length):
    p = Plan(sizes, rows, width, q_cols, kv_cols, length)
    lanes = p.per * rows
    blocks = p.reach + 1
    p.buf("tok", (rows, width), BF)
    p.buf("wq", (width, q_cols), BF)
    p.buf("wk", (width, kv_cols), BF)
    p.buf("wv", (width, kv_cols), BF)
    p.buf("cot", (rows, q_cols), BF)
    p.buf("seg", (1, length), jnp.int32)
    p.buf("kvb", (blocks, 2 * p.groups, rows, HEAD), BF)
    p.buf("qst", (p.groups, lanes, HEAD), BF)
    p.buf("dost", (p.groups, lanes, HEAD), BF)
    p.buf("bias", (blocks, rows, rows), F32)
    p.buf("s", (p.groups, blocks, rows, lanes), F32)
    p.buf("dp", (p.groups, blocks, rows, lanes), F32)
    p.buf("relay", (2, rows, HEAD), BF)
    p.buf("m", (p.groups, 8, lanes), F32)
    p.buf("top", (p.groups, 8, lanes), F32)
    p.buf("l", (p.groups, 8, lanes), F32)
    p.buf("de", (p.groups, 8, lanes), F32)
    p.buf("fac", (p.groups, 8, lanes), F32)
    p.buf("acc", (p.groups, blocks, 2, rows, HEAD), F32)
    p.buf("dqt", (p.groups, HEAD, lanes), F32)
    p.buf("relay_back", (p.groups, 2, rows, HEAD), BF)
    p.buf("far", (p.groups, 2, rows, HEAD), BF)
    p.buf("stage", (p.groups, blocks, 2, rows, HEAD), BF)
    p.buf("back", (p.groups, blocks, 2, rows, HEAD), BF)
    p.buf("tokt", (2, width // 2, rows), BF)
    p.buf("toktp", (width // 2, rows), BF)
    p.buf("dq", (rows, q_cols), BF)
    p.buf("dqp", (rows, q_cols), BF)
    p.buf("dkv", (p.groups, 2, rows, HEAD), BF)
    p.buf("dkvp", (p.groups, 2, rows, HEAD), BF)
    p.buf("gi32", (rows, width), F32)
    own, R = p.own, p.X
    for i, part in enumerate(p.parts):
        for j, (first, cols, x_first) in enumerate(part):
            for k, n, kind in (("one", R * own, BF), ("two", own, BF)):
                name = f"{k}{i}{j}"
                p.buf(name, (R, n, cols), kind)
                if i or k == "two":
                    p.buf(name + "got", (R - 1, n, cols), kind)
                    p.sem(name, 2, R)
                    continue
                p.buf(name + "up", (n, cols), kind)
                p.buf(name + "left", (n, cols), kind)
                p.buf(name + "right", (n, cols), kind)
                p.sem(name, 2, 3)
        tiles = own // 8 * sum(c for _, c, _ in part) // HEAD
        p.buf(f"zs{i}", (p.Z, tiles // p.Z * 8, HEAD), BF)
        p.buf(f"zr{i}", (p.Z, tiles // p.Z * 8, HEAD), BF)
        p.buf(f"zo{i}", (p.Z, tiles // p.Z * 8, HEAD), F32 if i else BF)
        p.sem(f"zr{i}", 2, p.Z)
        p.sem(f"zo{i}", 2, p.Z)
    p.sem("load", 6)
    p.sems["z_in"] = pltpu.SemaphoreType.REGULAR((2,))
    p.sem("ha", 2, 2 * p.groups)
    p.sem("hb", 2)
    p.sem("hc", 2, p.groups)
    p.sem("hd", 2)
    p.sem("he", 2)
    p.sem("hf", 2)
    p.sem("tokt", 2)
    p.sem("dq", 2)
    p.sem("dkv", 2, p.groups)
    p.sem("far", 2, p.groups, 2)
    p.sem("relay_back", 2, p.groups, 2)
    p.sem("ret", 2, p.groups, blocks)
    return p


def kernel(p, tok_h, wq_h, wk_h, wv_h, cot_h, seg_h, gi_ref, gq_ref, gk_ref, gv_ref, *refs):
    names = list(p.scratch)
    r = dict(zip(names, refs[: len(names)]))
    sm = dict(zip(p.sems, refs[len(names) :]))
    rows, lanes, blocks = p.rows, p.per * p.rows, p.reach + 1
    X, Y, Z, N, R = p.X, p.Y, p.Z, p.N, p.X
    z, me = lax.axis_index("dp"), lax.axis_index("ctx")
    core, chip = lax.rem(me, 2), me // 2
    cx, cy = chip // Y, lax.rem(chip, Y)
    peer = me + 1 - 2 * core
    nxt, prv = lax.rem(me + 2, N), lax.rem(me + N - 2, N)
    far_to = lax.rem(cx * Y + lax.rem(cy + 1, Y) + 2, p.chips) * 2 + core
    back2 = lax.rem(chip + p.chips - 2, p.chips)
    far_from = (back2 // Y * Y + lax.rem(lax.rem(back2, Y) + Y - 1, Y)) * 2 + core
    owner = lax.rem(cx * Y + lax.rem(cy + Y - 1, Y) + p.chips - 2, p.chips) * 2 + core
    ahead = lax.rem(chip + 2, p.chips)
    sender = (ahead // Y * Y + lax.rem(lax.rem(ahead, Y) + 1, Y)) * 2 + core
    scale = HEAD**-0.5

    def along_x(o):
        return (lax.rem(cx + o, X) * Y + cy) * 2 + core

    def along_y(o):
        return (cx * Y + lax.rem(cy + o, Y)) * 2 + core

    def remote(src, dst, send, recv, ctx, dp=None):
        return pltpu.make_async_remote_copy(
            src_ref=src, dst_ref=dst, send_sem=send, recv_sem=recv,
            device_id=(z if dp is None else dp, ctx), device_id_type=MESH,
        )

    loads = {}
    for i, (name, src) in enumerate(
        (("tok", tok_h), ("wk", wk_h), ("wv", wv_h), ("wq", wq_h), ("cot", cot_h), ("seg", seg_h))
    ):
        loads[name] = pltpu.make_async_copy(src, r[name], sm["load"].at[i])
        loads[name].start()
    barrier = pltpu.get_barrier_semaphore()

    def greet(ctx, dp):
        pl.semaphore_signal(barrier, inc=1, device_id=(dp, ctx), device_id_type=MESH)

    near_z = min(3, Z)
    for o in range(1, near_z):
        greet(me, lax.rem(z + o, Z))
        greet(me, lax.rem(z + Z - o, Z))
    ring = [along_x(o) for o in (1, X - 1)] + [along_y(o) for o in (1, Y - 1)]
    for d in [peer, nxt, prv, far_to, far_from, owner, sender] + ring:
        greet(d, z)

    def z_round(k, distance):
        if Z <= distance:
            return
        for to in (lax.rem(z + distance, Z), lax.rem(z + Z - distance, Z)):
            pl.semaphore_signal(sm["z_in"].at[k], inc=1, device_id=(to, me), device_id_type=MESH)

    def z_joined(k, distance):
        if Z > distance:
            pl.semaphore_wait(sm["z_in"].at[k], 2)

    mark("w_tok", lambda: [loads[name].wait() for name in ("tok", "wk", "wv")])
    for i, w in enumerate(("wk", "wv")):
        val = nn(r["tok"][...], r[w][...]).astype(BF)
        for g in range(p.groups):
            r["kvb"][0, i * p.groups + g] = val[:, g * HEAD : (g + 1) * HEAD]
    mark('w_bar', pl.semaphore_wait, barrier, 11 + 2 * (near_z - 1))
    z_round(0, 2)

    kvb = r["kvb"]

    G, both = p.groups, 2 * p.groups
    up = along_y(Y - 1)

    def pair(name, *at):
        x = sm[name]
        return x.at[(0, *at)], x.at[(1, *at)]

    def h_next(u):
        return remote(kvb.at[0, u], kvb.at[2, u], *pair("ha", u), nxt)

    def h_one(src):
        return remote(kvb.at[src], kvb.at[1], *pair("hb"), peer)

    def h_four(u):
        return remote(kvb.at[2, u], kvb.at[4, u], *pair("hc", u), nxt)

    def h_three(src):
        return remote(kvb.at[src], kvb.at[3], *pair("hd"), peer)

    far_one = remote(kvb.at[0, pl.ds(G, G)], r["relay"], *pair("he"), up)
    far_two = remote(r["relay"], kvb.at[4, pl.ds(G, G)], *pair("hf"), far_to)
    h_next(0).start()
    far_one.start()
    for u in range(1, both):
        h_next(u).start()

    @pl.when(core == 0)
    def _():
        h_one(0).start()

    mark("w_wq", loads["wq"].wait)
    step = 2 * HEAD
    for n in range(p.q_cols // step):
        val = nn(r["tok"][...], r["wq"][:, n * step : (n + 1) * step]).astype(BF)
        for j in range(2):
            g, h = divmod(2 * n + j, p.per)
            r["qst"][g, h * rows : (h + 1) * rows] = val[:, j * HEAD : (j + 1) * HEAD]
    mark("w_cot", loads["cot"].wait)
    for n in range(p.heads):
        g, h = divmod(n, p.per)
        r["dost"][g, h * rows : (h + 1) * rows] = r["cot"][:, n * HEAD : (n + 1) * HEAD]

    mark("w_seg", loads["seg"].wait)
    start = me * rows
    seg = r["seg"][...]
    q_seg = r["seg"][:, pl.ds(pl.multiple_of(start, rows), rows)]
    doc = jnp.zeros((1, rows), jnp.int32)
    for t in range(1, 4):
        below = jnp.sum((seg < t).astype(F32), axis=1, keepdims=True)
        doc = jnp.where(q_seg >= t, below.astype(jnp.int32), doc)
    row = lax.broadcasted_iota(jnp.int32, (rows, rows), 0)
    col = lax.broadcasted_iota(jnp.int32, (rows, rows), 1)
    for b in range(blocks):
        j = row + (start - b * rows)
        gap = col - row + b * rows
        ok = (j >= doc) & (gap >= 0) & (gap < WINDOW)
        r["bias"][b] = jnp.where(ok, 0.0, NEG)

    for n in range(p.width // HEAD):
        val = r["tok"][:, n * HEAD : (n + 1) * HEAD].astype(F32).T.astype(BF)
        for k in range(HEAD // p.own):
            ch, c = divmod(n * (HEAD // p.own) + k, 2)
            r["tokt"][c, ch * p.own : (ch + 1) * p.own] = val[k * p.own : (k + 1) * p.own]
    tokt_copy = remote(r["tokt"].at[1 - core], r["toktp"], sm["tokt"].at[0], sm["tokt"].at[1], peer)
    tokt_copy.start()

    r["m"][...] = jnp.full(r["m"].shape, -3e38, F32)

    def pass1(b):
        def body(g, c):
            kk, vv = kvb[b, g], kvb[b, p.groups + g]
            for h in range(p.per):
                cols = slice(h * rows, (h + 1) * rows)
                s = nt(kk, r["qst"][g, cols]) + r["bias"][b]
                r["s"][g, b, :, cols] = s
                r["m"][g, :, cols] = jnp.maximum(
                    r["m"][g, :, cols], jnp.max(s.reshape(rows // 8, 8, rows), axis=0)
                )
                r["dp"][g, b, :, cols] = nt(vv, r["dost"][g, cols])
            return c

        lax.fori_loop(0, p.groups, body, 0)

    mark("pass1_0", pass1, 0)
    for u in range(G):
        mark("w_next", h_next(u).wait_recv)
        h_four(u).start()
    mark("w_far", far_one.wait_recv)
    far_two.start()
    for u in range(G, both):
        mark("w_next2", h_next(u).wait_recv)

    @pl.when(core == 0)
    def _():
        h_three(2).start()

    @pl.when(core == 1)
    def _():
        h_one(2).start()

    mark("pass1_2", pass1, 2)
    mark("w_one", h_one(0).wait_recv)
    mark("pass1_1", pass1, 1)

    r["l"][...] = jnp.zeros(r["l"].shape, F32)
    r["de"][...] = jnp.zeros(r["de"].shape, F32)

    def expo(g, b):
        for h in range(p.per):
            cols = slice(h * rows, (h + 1) * rows)
            e = jnp.exp((r["s"][g, b, :, cols] - r["top"][g, 0:1, cols]) * scale)
            r["s"][g, b, :, cols] = e
            r["l"][g, :, cols] += jnp.sum(e.reshape(rows // 8, 8, rows), axis=0)
            de = e * r["dp"][g, b, :, cols]
            r["de"][g, :, cols] += jnp.sum(de.reshape(rows // 8, 8, rows), axis=0)

    def early(g, c):
        r["top"][g] = jnp.broadcast_to(jnp.max(r["m"][g], axis=0, keepdims=True), (8, lanes))

        def one(b, c2):
            expo(g, b)
            return c2

        return lax.fori_loop(0, 3, one, c)

    def late(g, c):
        top = jnp.broadcast_to(jnp.max(r["m"][g], axis=0, keepdims=True), (8, lanes))
        down = jnp.exp((r["top"][g] - top) * scale)
        r["top"][g] = top
        r["fac"][g] = down
        r["l"][g] *= down
        r["de"][g] *= down

        def one(b, c2):
            expo(g, b)
            return c2

        lax.fori_loop(3, blocks, one, c)
        inv = 1.0 / jnp.sum(r["l"][g], axis=0, keepdims=True)
        delta = jnp.sum(r["de"][g], axis=0, keepdims=True) * inv
        r["l"][g] = jnp.broadcast_to(inv, (8, lanes))
        r["de"][g] = jnp.broadcast_to(delta, (8, lanes))
        return c

    z_joined(0, 2)
    z_round(1, 4)
    mark("early", lax.fori_loop, 0, G, early, 0)
    for u in range(G):
        mark("w_four", h_four(u).wait_recv)
    mark("w_far2", far_two.wait_recv)

    @pl.when(core == 1)
    def _():
        h_three(4).start()

    mark("pass1_4", pass1, 4)
    mark("w_three", h_three(2).wait_recv)
    mark("pass1_3", pass1, 3)
    mark("late", lax.fori_loop, 0, G, late, 0)

    acc, stage, back = r["acc"], r["stage"], r["back"]
    first_core = (core == 0).astype(F32)
    second_core = (core == 1).astype(F32)
    r["dqt"][...] = jnp.zeros(r["dqt"].shape, F32)

    def grads(b):
        def body(g, c):
            kk = kvb[b, g]
            dv = jnp.zeros((rows, HEAD), F32)
            dk = jnp.zeros((rows, HEAD), F32)
            for h in range(p.per):
                cols = slice(h * rows, (h + 1) * rows)
                inv = r["l"][g, 0:1, cols]
                if b < 3:
                    inv = inv * r["fac"][g, 0:1, cols]
                prob = r["s"][g, b, :, cols] * inv
                ds = (prob * (r["dp"][g, b, :, cols] - r["de"][g, 0:1, cols]) * scale).astype(BF)
                dv = dv + nn(prob.astype(BF), r["dost"][g, cols])
                dk = dk + nn(ds, r["qst"][g, cols])
                r["dqt"][g, :, cols] += tn(kk, ds)
            acc[g, b, 0] = dk
            acc[g, b, 1] = dv
            if b in (1, 3, 4):
                stage[g, b, 0] = dk.astype(BF)
                stage[g, b, 1] = dv.astype(BF)
            return c

        lax.fori_loop(0, G, body, 0)

    def ret(g, d, to):
        return remote(stage.at[g, d], back.at[g, d], *pair("ret", g, d), to)

    units = [(g, i) for g in range(G) for i in range(2)]

    def far_send(g, i):
        to = prv if (g, i) == (0, 0) else along_y(1)
        return remote(stage.at[g, 4, i], r["relay_back"].at[g, i], *pair("relay_back", g, i), to)

    def far_last(g, i):
        to = prv if (g, i) == (0, 0) else owner
        return remote(r["relay_back"].at[g, i], r["far"].at[g, i], *pair("far", g, i), to)

    def to_peer(d):
        for g in range(G):
            ret(g, d, peer).start()

    def ret4(g):
        @pl.when(core == 1)
        def _():
            ret(g, 3, peer).wait_recv()
            stage[g, 4] = (acc[g, 4] + back[g, 3].astype(F32)).astype(BF)

        for i in range(2):
            far_send(g, i).start()

    def forward_far(g, i):
        far_send(g, i).wait_recv()
        far_last(g, i).start()

    def ret2(g):
        @pl.when(core == 0)
        def _():
            ret(g, 3, peer).wait_recv()

        ret(g, 1, peer).wait_recv()
        t = acc[g, 2] + first_core * back[g, 3].astype(F32) + second_core * back[g, 1].astype(F32)
        stage[g, 2] = t.astype(BF)
        ret(g, 2, prv).start()

    def dkv_copy(g):
        return remote(r["dkv"].at[g], r["dkvp"].at[g], *pair("dkv", g), peer)

    def ret0(g):
        ret(g, 2, prv).wait_recv()
        for i in range(2):
            far_last(g, i).wait_recv()
        t = acc[g, 0] + back[g, 2].astype(F32) + first_core * back[g, 1].astype(F32)
        r["dkv"][g] = (t + r["far"][g].astype(F32)).astype(BF)
        dkv_copy(g).start()

    def made(one, x_first, at, mine, other):
        val = (nn(r["tokt"][core], mine) + nn(r["toktp"][...], other)).astype(BF)
        if x_first:
            one[:, :, at] = val.reshape(X, Y * p.own, val.shape[1])
        else:
            for a in range(X):
                for k in range(Y):
                    ro = (a * Y + k) * p.own
                    one[k, a * p.own : (a + 1) * p.own, at] = val[ro : ro + p.own]

    def made_q(j):
        first, cols, x_first = p.parts[0][j]

        def body(n, c):
            to = pl.ds(pl.multiple_of(n * step, step), step)
            at = pl.ds(pl.multiple_of(first + n * step, step), step)
            made(r[f"one0{j}"], x_first, to, r["dq"][:, at], r["dqp"][:, at])
            return c

        lax.fori_loop(0, cols // step, body, 0)

    def made_kv(j):
        def wide(name):
            return jnp.concatenate([r[name][g, j] for g in range(G)], axis=1)

        made(r[f"one1{j}"], p.parts[1][j][2], slice(0, p.kv_cols), wide("dkv"), wide("dkvp"))

    class Ring:
        def __init__(self, k, i, j):
            x_first = p.parts[i][j][2]
            on_x = x_first == (k == "one")
            self.name = f"{k}{i}{j}"
            self.at, along = (cx, along_x) if on_x else (cy, along_y)
            self.next, self.prev, self.along = along(1), along(R - 1), along

        def chunk(self, o):
            return r[self.name].at[lax.rem(self.at + o, R)]

        def copy(self, k, src, dst, to):
            return remote(src, dst, *pair(self.name, k), to)

        def two_up(self):
            return self.copy(0, self.chunk(2), r[self.name + "up"], self.next)

        def up(self):
            return self.copy(1, self.chunk(1), r[self.name + "left"], self.next)

        def down(self):
            return self.copy(2, self.chunk(R - 1), r[self.name + "right"], self.prev)

        def pass_up(self):
            self.two_up().wait_recv()
            k = lax.rem(self.at + 1, R)
            val = r[self.name][k].astype(F32) + r[self.name + "up"][...].astype(F32)
            r[self.name][k] = val.astype(BF)
            self.up().start()

        def copies(self):
            return [self.two_up(), self.up(), self.down()]

        def total(self):
            self.up().wait_recv()
            self.down().wait_recv()
            t = r[self.name][self.at].astype(F32)
            return t + r[self.name + "left"][...].astype(F32) + r[self.name + "right"][...].astype(F32)

    class Direct(Ring):
        def copies(self):
            for o in range(1, R):
                to = self.along(o)
                yield self.copy(o, self.chunk(o), r[self.name + "got"].at[o - 1], to)

        def start(self):
            for copy in self.copies():
                copy.start()

        def total(self):
            t = r[self.name][self.at].astype(F32)
            for o, copy in enumerate(self.copies()):
                copy.wait_recv()
                t = t + r[self.name + "got"][o].astype(F32)
            return t

    kinds = (Ring, Direct)
    one = [[kinds[i]("one", i, j) for j in range(2)] for i in range(2)]
    two = [[Direct("two", i, j) for j in range(2)] for i in range(2)]

    def start_second(i):
        for j in range(2):
            t = one[i][j].total()
            r[f"two{i}{j}"][...] = t.reshape(R, p.own, t.shape[1]).astype(r[f"two{i}{j}"].dtype)
            two[i][j].start()

    def z_hop(i, o):
        to = lax.rem(z + o, Z)
        s = sm[f"zr{i}"]
        return remote(r[f"zs{i}"].at[to], r[f"zr{i}"].at[o], s.at[0, o], s.at[1, o], me, to)

    def z_gather(i, o):
        to = lax.rem(z + o, Z)
        s = sm[f"zo{i}"]
        return remote(r[f"zo{i}"].at[z], r[f"zo{i}"].at[z], s.at[0, o], s.at[1, o], me, to)

    def loop_z(f):
        def body(k, c):
            f(Z // 2 + (k + 1) // 2 * (1 - 2 * lax.rem(k, 2)))
            return c

        lax.fori_loop(0, Z - 1, body, 0)

    def tiles_of(i):
        per_z = r[f"zs{i}"].shape[1] // 8
        ncb = sum(c for _, c, _ in p.parts[i]) // HEAD
        for t in range(per_z * Z):
            yield t // per_z, (t % per_z) * 8, (t // ncb) * 8, (t % ncb) * HEAD

    def start_z(i):
        pieces = [two[i][j].total() for j in range(2)]
        width = pieces[0].shape[1]
        for zi, zr, ro, co in tiles_of(i):
            part = pieces[co // width]
            co = co % width
            r[f"zs{i}"][zi, zr : zr + 8] = part[ro : ro + 8, co : co + HEAD].astype(BF)
        loop_z(lambda o: z_hop(i, o).start())

    def start_gather(i):
        loop_z(lambda o: z_hop(i, o).wait_recv())
        t = r[f"zs{i}"][z].astype(F32)
        for o in range(1, Z):
            t = t + r[f"zr{i}"][o].astype(F32)
        r[f"zo{i}"][z] = (t * ((Z * N * rows) ** -0.5)).astype(r[f"zo{i}"].dtype)
        loop_z(lambda o: z_gather(i, o).start())

    def finish(i):
        loop_z(lambda o: z_gather(i, o).wait_recv())
        for zi, zr, ro, co in tiles_of(i):
            val = r[f"zo{i}"][zi, zr : zr + 8].astype(F32)
            if i == 0:
                gq_ref[ro : ro + 8, co : co + HEAD] = val
            elif co < p.kv_cols:
                gk_ref[ro : ro + 8, co : co + HEAD] = val
            else:
                gv_ref[ro : ro + 8, co - p.kv_cols : co - p.kv_cols + HEAD] = val

    z_joined(1, 4)
    mark("grads3", grads, 3)
    to_peer(3)
    mark("grads1", grads, 1)
    to_peer(1)
    mark("grads4", grads, 4)
    mark("ret4", lambda: [ret4(g) for g in range(G)])
    mark("grads2", grads, 2)
    mark("ret2", lambda: [ret2(g) for g in range(G)])
    mark("grads0", grads, 0)

    def dq_rows():
        for n in range(p.heads):
            g, h = divmod(n, p.per)
            r["dq"][:, n * HEAD : (n + 1) * HEAD] = r["dqt"][g, :, h * rows : (h + 1) * rows].T.astype(BF)

    mark("dq_rows", dq_rows)
    dq_copy = remote(r["dq"], r["dqp"], *pair("dq"), peer)
    dq_copy.start()
    def gi_q(n, c):
        at = pl.ds(pl.multiple_of(n * step, step), step)
        r["gi32"][:, at] = nt(r["dq"][...], r["wq"][at])
        return c

    mark("gi_q", lax.fori_loop, 0, p.width // step, gi_q, 0)
    mark("fwd_far", lambda: [forward_far(0, i) for i in range(2)])
    mark("w_dq", lambda: (tokt_copy.wait_recv(), dq_copy.wait_recv()))
    mark("made_q", made_q, 0)
    one[0][0].two_up().start()
    mark("fwd_far2", forward_far, 1, 0)
    mark("made_q", made_q, 1)
    one[0][1].two_up().start()
    mark("fwd_far2", forward_far, 1, 1)

    mark("pass_q", one[0][0].pass_up)
    mark("ret0_0", ret0, 0)
    one[0][0].down().start()
    mark("ret0_1", ret0, 1)
    one[0][1].down().start()
    mark("pass_q", one[0][1].pass_up)
    mark("w_dkv", lambda: [dkv_copy(g).wait_recv() for g in range(G)])
    for j in range(2):
        mark("made_kv", made_kv, j)
        one[1][j].start()

    def gi_kv(n, c):
        at = pl.ds(pl.multiple_of(n * step, step), step)
        val = r["gi32"][:, at]
        for i, w in enumerate(("wk", "wv")):
            for g in range(G):
                val = val + nt(r["dkv"][g, i], r[w][at, g * HEAD : (g + 1) * HEAD])
        gi_ref[:, at] = val.astype(BF)
        return c

    mark("second_0", start_second, 0)
    mark("gi_kv", lax.fori_loop, 0, p.width // step, gi_kv, 0)
    mark("second_1", start_second, 1)
    mark("z_0", start_z, 0)
    mark("z_1", start_z, 1)
    mark("gather_0", start_gather, 0)
    mark("gather_1", start_gather, 1)
    mark("finish_0", finish, 0)
    mark("finish_1", finish, 1)

    for u in range(both):
        h_next(u).wait_send()
    for u in range(G):
        h_four(u).wait_send()
    for copy in (h_one(0), h_three(2), far_one, far_two, tokt_copy, dq_copy):
        copy.wait_send()
    for g in range(G):
        for copy in (ret(g, 3, peer), ret(g, 1, peer), ret(g, 2, prv), dkv_copy(g)):
            copy.wait_send()
    for unit in units:
        far_send(*unit).wait_send()
        far_last(*unit).wait_send()
    for i in range(2):
        for ring_sum in one[i] + two[i]:
            for copy in ring_sum.copies():
                copy.wait_send()
        loop_z(lambda o: z_hop(i, o).wait_send())
        loop_z(lambda o: z_gather(i, o).wait_send())


def emit(*refs):
    n = (len(refs) - 1) // 2
    copies = [pltpu.make_async_copy(refs[i], refs[n + i], refs[-1].at[i]) for i in range(n)]
    for c in copies:
        c.start()
    for c in copies:
        c.wait()


def body(sizes, tokens, w_query, key_weight, value_weight, cotangent, segment_ids):
    rows, width = tokens.shape[1:]
    q_cols, kv_cols = w_query.shape[1], key_weight.shape[1]
    p = build_plan(sizes, rows, width, q_cols, kv_cols, segment_ids.shape[1])
    anyspace = pl.BlockSpec(memory_space=pl.ANY)
    vmem = pl.BlockSpec(memory_space=pltpu.VMEM)
    shapes = (
        jax.ShapeDtypeStruct((rows, width), BF),
        jax.ShapeDtypeStruct((p.own, q_cols), F32),
        jax.ShapeDtypeStruct((p.own, kv_cols), F32),
        jax.ShapeDtypeStruct((p.own, kv_cols), F32),
    )
    out = pl.pallas_call(
        functools.partial(kernel, p),
        out_shape=shapes,
        in_specs=[anyspace] * 6,
        out_specs=(vmem,) * 4,
        scratch_shapes=list(p.scratch.values()) + list(p.sems.values()),
        compiler_params=pltpu.CompilerParams(
            collective_id=0, has_side_effects=True, vmem_limit_bytes=VMEM_LIMIT
        ),
        name="step",
    )(tokens[0], w_query, key_weight, value_weight, cotangent[0], segment_ids)
    out = pl.pallas_call(
        emit,
        out_shape=shapes,
        in_specs=[vmem] * 4,
        out_specs=(anyspace,) * 4,
        scratch_shapes=[pltpu.SemaphoreType.DMA((4,))],
        name="emit",
    )(*out)
    return out[0][None], out[1], out[2], out[3]


def solution(mesh):
    sizes = dict(mesh.shape)
    placed = (P("dp", "ctx", None), P(), P(), P(), P("dp", "ctx", None), P("dp", None))
    return jax.shard_map(
        functools.partial(body, sizes),
        mesh=mesh,
        in_specs=placed,
        out_specs=(P("dp", "ctx", None), P("ctx", None), P("ctx", None), P("ctx", None)),
        check_vma=False,
    )
```

```python
import functools
import math

import jax
import jax.numpy as jnp
from jax import lax
from jax.experimental import pallas as pl
from jax.experimental.pallas import tpu as pltpu
from jax.sharding import PartitionSpec as P

HEAD = 128
WINDOW = 1024
NEG = -1e30
VMEM_LIMIT = 54 * 1024 * 1024
BF = jnp.bfloat16
F32 = jnp.float32
MESH = pl.DeviceIdType.MESH
TRACE = False


def mark(name, f, *a):
    if not TRACE:
        return f(*a)
    with jax.named_scope(name):
        return f(*a)


def nn(a, b):
    return lax.dot_general(a, b, (((1,), (0,)), ((), ())), preferred_element_type=F32)


def nt(a, b):
    return lax.dot_general(a, b, (((1,), (1,)), ((), ())), preferred_element_type=F32)


def tn(a, b):
    return lax.dot_general(a, b, (((0,), (0,)), ((), ())), preferred_element_type=F32)


class Plan:
    def __init__(self, sizes, rows, width, q_cols, kv_cols, length):
        self.Z, self.N = sizes["dp"], sizes["ctx"]
        self.X = self.Y = math.isqrt(self.N // 2)
        self.rows, self.width, self.q_cols, self.kv_cols = rows, width, q_cols, kv_cols
        self.length = length
        self.heads = q_cols // HEAD
        self.groups = kv_cols // HEAD
        self.per = self.heads // self.groups
        self.reach = WINDOW // rows
        self.chips = self.N // 2
        self.own = width // self.N
        half = q_cols // 2
        self.q_pieces = ((0, half, True), (half, half, True))
        self.kv_pieces = ((q_cols, kv_cols, True), (q_cols + kv_cols, kv_cols, False))
        self.parts = (self.q_pieces, self.kv_pieces)
        self.scratch = {}
        self.sems = {}

    def buf(self, name, shape, dtype):
        self.scratch[name] = pltpu.VMEM(shape, dtype)

    def sem(self, name, *shape):
        self.sems[name] = pltpu.SemaphoreType.DMA(shape)


def build_plan(sizes, rows, width, q_cols, kv_cols, length):
    p = Plan(sizes, rows, width, q_cols, kv_cols, length)
    lanes = p.per * rows
    blocks = p.reach + 1
    p.buf("tok", (rows, width), BF)
    p.buf("wq", (width, q_cols), BF)
    p.buf("wk", (width, kv_cols), BF)
    p.buf("wv", (width, kv_cols), BF)
    p.buf("cot", (rows, q_cols), BF)
    p.buf("seg", (1, length), jnp.int32)
    p.buf("kvb", (blocks, 2 * p.groups, rows, HEAD), BF)
    p.buf("qst", (p.groups, lanes, HEAD), BF)
    p.buf("dost", (p.groups, lanes, HEAD), BF)
    p.buf("bias", (blocks, rows, rows), F32)
    p.buf("s", (p.groups, blocks, rows, lanes), F32)
    p.buf("dp", (p.groups, blocks, rows, lanes), F32)
    p.buf("relay", (2, rows, HEAD), BF)
    p.buf("m", (p.groups, 8, lanes), F32)
    p.buf("top", (p.groups, 8, lanes), F32)
    p.buf("l", (p.groups, 8, lanes), F32)
    p.buf("de", (p.groups, 8, lanes), F32)
    p.buf("fac", (p.groups, 8, lanes), F32)
    p.buf("acc", (p.groups, blocks, 2, rows, HEAD), F32)
    p.buf("dqt", (p.groups, HEAD, lanes), F32)
    p.buf("relay_back", (p.groups, 2, rows, HEAD), BF)
    p.buf("far", (p.groups, 2, rows, HEAD), BF)
    p.buf("stage", (p.groups, blocks, 2, rows, HEAD), BF)
    p.buf("back", (p.groups, blocks, 2, rows, HEAD), BF)
    p.buf("tokt", (2, width // 2, rows), BF)
    p.buf("toktp", (width // 2, rows), BF)
    p.buf("dq", (rows, q_cols), BF)
    p.buf("dqp", (rows, q_cols), BF)
    p.buf("dkv", (p.groups, 2, rows, HEAD), BF)
    p.buf("dkvp", (p.groups, 2, rows, HEAD), BF)
    p.buf("gi32", (rows, width), F32)
    own, R = p.own, p.X
    for i, part in enumerate(p.parts):
        for j, (first, cols, x_first) in enumerate(part):
            for k, n, kind in (("one", R * own, BF), ("two", own, BF)):
                name = f"{k}{i}{j}"
                p.buf(name, (R, n, cols), kind)
                if i or k == "two":
                    p.buf(name + "got", (R - 1, n, cols), kind)
                    p.sem(name, 2, R)
                    continue
                p.buf(name + "up", (n, cols), kind)
                p.buf(name + "left", (n, cols), kind)
                p.buf(name + "right", (n, cols), kind)
                p.sem(name, 2, 3)
        tiles = own // 8 * sum(c for _, c, _ in part) // HEAD
        p.buf(f"zs{i}", (p.Z, tiles // p.Z * 8, HEAD), BF)
        p.buf(f"zr{i}", (p.Z, tiles // p.Z * 8, HEAD), BF)
        p.buf(f"zo{i}", (p.Z, tiles // p.Z * 8, HEAD), F32 if i else BF)
        p.sem(f"zr{i}", 2, p.Z)
        p.sem(f"zo{i}", 2, p.Z)
    p.sem("load", 6)
    p.sems["z_in"] = pltpu.SemaphoreType.REGULAR((2,))
    p.sem("ha", 2, 2 * p.groups)
    p.sem("hb", 2)
    p.sem("hc", 2, p.groups)
    p.sem("hd", 2)
    p.sem("he", 2)
    p.sem("hf", 2)
    p.sem("tokt", 2)
    p.sem("dq", 2)
    p.sem("dkv", 2, p.groups)
    p.sem("far", 2, p.groups, 2)
    p.sem("relay_back", 2, p.groups, 2)
    p.sem("ret", 2, p.groups, blocks)
    return p


def kernel(p, tok_h, wq_h, wk_h, wv_h, cot_h, seg_h, gi_ref, gq_ref, gk_ref, gv_ref, *refs):
    names = list(p.scratch)
    r = dict(zip(names, refs[: len(names)]))
    sm = dict(zip(p.sems, refs[len(names) :]))
    rows, lanes, blocks = p.rows, p.per * p.rows, p.reach + 1
    X, Y, Z, N, R = p.X, p.Y, p.Z, p.N, p.X
    z, me = lax.axis_index("dp"), lax.axis_index("ctx")
    core, chip = lax.rem(me, 2), me // 2
    cx, cy = chip // Y, lax.rem(chip, Y)
    peer = me + 1 - 2 * core
    nxt, prv = lax.rem(me + 2, N), lax.rem(me + N - 2, N)
    far_to = lax.rem(cx * Y + lax.rem(cy + 1, Y) + 2, p.chips) * 2 + core
    back2 = lax.rem(chip + p.chips - 2, p.chips)
    far_from = (back2 // Y * Y + lax.rem(lax.rem(back2, Y) + Y - 1, Y)) * 2 + core
    owner = lax.rem(cx * Y + lax.rem(cy + Y - 1, Y) + p.chips - 2, p.chips) * 2 + core
    ahead = lax.rem(chip + 2, p.chips)
    sender = (ahead // Y * Y + lax.rem(lax.rem(ahead, Y) + 1, Y)) * 2 + core
    scale = HEAD**-0.5

    def along_x(o):
        return (lax.rem(cx + o, X) * Y + cy) * 2 + core

    def along_y(o):
        return (cx * Y + lax.rem(cy + o, Y)) * 2 + core

    def remote(src, dst, send, recv, ctx, dp=None):
        return pltpu.make_async_remote_copy(
            src_ref=src, dst_ref=dst, send_sem=send, recv_sem=recv,
            device_id=(z if dp is None else dp, ctx), device_id_type=MESH,
        )

    loads = {}
    for i, (name, src) in enumerate(
        (("tok", tok_h), ("wk", wk_h), ("wv", wv_h), ("wq", wq_h), ("cot", cot_h), ("seg", seg_h))
    ):
        loads[name] = pltpu.make_async_copy(src, r[name], sm["load"].at[i])
        loads[name].start()
    barrier = pltpu.get_barrier_semaphore()

    def greet(ctx, dp):
        pl.semaphore_signal(barrier, inc=1, device_id=(dp, ctx), device_id_type=MESH)

    near_z = min(3, Z)
    for o in range(1, near_z):
        greet(me, lax.rem(z + o, Z))
        greet(me, lax.rem(z + Z - o, Z))
    ring = [along_x(o) for o in (1, X - 1)] + [along_y(o) for o in (1, Y - 1)]
    for d in [peer, nxt, prv, far_to, far_from, owner, sender] + ring:
        greet(d, z)

    def z_round(k, distance):
        if Z <= distance:
            return
        for to in (lax.rem(z + distance, Z), lax.rem(z + Z - distance, Z)):
            pl.semaphore_signal(sm["z_in"].at[k], inc=1, device_id=(to, me), device_id_type=MESH)

    def z_joined(k, distance):
        if Z > distance:
            pl.semaphore_wait(sm["z_in"].at[k], 2)

    mark("w_tok", lambda: [loads[name].wait() for name in ("tok", "wk", "wv")])
    for i, w in enumerate(("wk", "wv")):
        val = nn(r["tok"][...], r[w][...]).astype(BF)
        for g in range(p.groups):
            r["kvb"][0, i * p.groups + g] = val[:, g * HEAD : (g + 1) * HEAD]
    mark('w_bar', pl.semaphore_wait, barrier, 11 + 2 * (near_z - 1))
    z_round(0, 2)

    kvb = r["kvb"]

    G, both = p.groups, 2 * p.groups
    up = along_y(Y - 1)

    def pair(name, *at):
        x = sm[name]
        return x.at[(0, *at)], x.at[(1, *at)]

    def h_next(u):
        return remote(kvb.at[0, u], kvb.at[2, u], *pair("ha", u), nxt)

    def h_one(src):
        return remote(kvb.at[src], kvb.at[1], *pair("hb"), peer)

    def h_four(u):
        return remote(kvb.at[2, u], kvb.at[4, u], *pair("hc", u), nxt)

    def h_three(src):
        return remote(kvb.at[src], kvb.at[3], *pair("hd"), peer)

    far_one = remote(kvb.at[0, pl.ds(G, G)], r["relay"], *pair("he"), up)
    far_two = remote(r["relay"], kvb.at[4, pl.ds(G, G)], *pair("hf"), far_to)
    h_next(0).start()
    far_one.start()
    for u in range(1, both):
        h_next(u).start()

    @pl.when(core == 0)
    def _():
        h_one(0).start()

    mark("w_wq", loads["wq"].wait)
    step = 2 * HEAD
    for n in range(p.q_cols // step):
        val = nn(r["tok"][...], r["wq"][:, n * step : (n + 1) * step]).astype(BF)
        for j in range(2):
            g, h = divmod(2 * n + j, p.per)
            r["qst"][g, h * rows : (h + 1) * rows] = val[:, j * HEAD : (j + 1) * HEAD]
    mark("w_cot", loads["cot"].wait)
    for n in range(p.heads):
        g, h = divmod(n, p.per)
        r["dost"][g, h * rows : (h + 1) * rows] = r["cot"][:, n * HEAD : (n + 1) * HEAD]

    mark("w_seg", loads["seg"].wait)
    start = me * rows
    seg = r["seg"][...]
    q_seg = r["seg"][:, pl.ds(pl.multiple_of(start, rows), rows)]
    doc = jnp.zeros((1, rows), jnp.int32)
    for t in range(1, 4):
        below = jnp.sum((seg < t).astype(F32), axis=1, keepdims=True)
        doc = jnp.where(q_seg >= t, below.astype(jnp.int32), doc)
    row = lax.broadcasted_iota(jnp.int32, (rows, rows), 0)
    col = lax.broadcasted_iota(jnp.int32, (rows, rows), 1)
    for b in range(blocks):
        j = row + (start - b * rows)
        gap = col - row + b * rows
        ok = (j >= doc) & (gap >= 0) & (gap < WINDOW)
        r["bias"][b] = jnp.where(ok, 0.0, NEG)

    for n in range(p.width // HEAD):
        val = r["tok"][:, n * HEAD : (n + 1) * HEAD].astype(F32).T.astype(BF)
        for k in range(HEAD // p.own):
            ch, c = divmod(n * (HEAD // p.own) + k, 2)
            r["tokt"][c, ch * p.own : (ch + 1) * p.own] = val[k * p.own : (k + 1) * p.own]
    tokt_copy = remote(r["tokt"].at[1 - core], r["toktp"], sm["tokt"].at[0], sm["tokt"].at[1], peer)
    tokt_copy.start()

    r["m"][...] = jnp.full(r["m"].shape, -3e38, F32)

    def pass1(b):
        def body(g, c):
            kk, vv = kvb[b, g], kvb[b, p.groups + g]
            for h in range(p.per):
                cols = slice(h * rows, (h + 1) * rows)
                s = nt(kk, r["qst"][g, cols]) + r["bias"][b]
                r["s"][g, b, :, cols] = s
                r["m"][g, :, cols] = jnp.maximum(
                    r["m"][g, :, cols], jnp.max(s.reshape(rows // 8, 8, rows), axis=0)
                )
                r["dp"][g, b, :, cols] = nt(vv, r["dost"][g, cols])
            return c

        lax.fori_loop(0, p.groups, body, 0)

    mark("pass1_0", pass1, 0)
    for u in range(G):
        mark("w_next", h_next(u).wait_recv)
        h_four(u).start()
    mark("w_far", far_one.wait_recv)
    far_two.start()
    for u in range(G, both):
        mark("w_next2", h_next(u).wait_recv)

    @pl.when(core == 0)
    def _():
        h_three(2).start()

    @pl.when(core == 1)
    def _():
        h_one(2).start()

    mark("pass1_2", pass1, 2)
    mark("w_one", h_one(0).wait_recv)
    mark("pass1_1", pass1, 1)

    r["l"][...] = jnp.zeros(r["l"].shape, F32)
    r["de"][...] = jnp.zeros(r["de"].shape, F32)

    def expo(g, b):
        for h in range(p.per):
            cols = slice(h * rows, (h + 1) * rows)
            e = jnp.exp((r["s"][g, b, :, cols] - r["top"][g, 0:1, cols]) * scale)
            r["s"][g, b, :, cols] = e
            r["l"][g, :, cols] += jnp.sum(e.reshape(rows // 8, 8, rows), axis=0)
            de = e * r["dp"][g, b, :, cols]
            r["de"][g, :, cols] += jnp.sum(de.reshape(rows // 8, 8, rows), axis=0)

    def early(g, c):
        r["top"][g] = jnp.broadcast_to(jnp.max(r["m"][g], axis=0, keepdims=True), (8, lanes))

        def one(b, c2):
            expo(g, b)
            return c2

        return lax.fori_loop(0, 3, one, c)

    def late(g, c):
        top = jnp.broadcast_to(jnp.max(r["m"][g], axis=0, keepdims=True), (8, lanes))
        down = jnp.exp((r["top"][g] - top) * scale)
        r["top"][g] = top
        r["fac"][g] = down
        r["l"][g] *= down
        r["de"][g] *= down

        def one(b, c2):
            expo(g, b)
            return c2

        lax.fori_loop(3, blocks, one, c)
        inv = 1.0 / jnp.sum(r["l"][g], axis=0, keepdims=True)
        delta = jnp.sum(r["de"][g], axis=0, keepdims=True) * inv
        r["l"][g] = jnp.broadcast_to(inv, (8, lanes))
        r["de"][g] = jnp.broadcast_to(delta, (8, lanes))
        return c

    z_joined(0, 2)
    z_round(1, 4)
    mark("early", lax.fori_loop, 0, G, early, 0)
    for u in range(G):
        mark("w_four", h_four(u).wait_recv)
    mark("w_far2", far_two.wait_recv)

    @pl.when(core == 1)
    def _():
        h_three(4).start()

    mark("pass1_4", pass1, 4)
    mark("w_three", h_three(2).wait_recv)
    mark("pass1_3", pass1, 3)
    mark("late", lax.fori_loop, 0, G, late, 0)

    acc, stage, back = r["acc"], r["stage"], r["back"]
    first_core = (core == 0).astype(F32)
    second_core = (core == 1).astype(F32)
    r["dqt"][...] = jnp.zeros(r["dqt"].shape, F32)

    def grads(b):
        def body(g, c):
            kk = kvb[b, g]
            dv = jnp.zeros((rows, HEAD), F32)
            dk = jnp.zeros((rows, HEAD), F32)
            for h in range(p.per):
                cols = slice(h * rows, (h + 1) * rows)
                inv = r["l"][g, 0:1, cols]
                if b < 3:
                    inv = inv * r["fac"][g, 0:1, cols]
                prob = r["s"][g, b, :, cols] * inv
                ds = (prob * (r["dp"][g, b, :, cols] - r["de"][g, 0:1, cols]) * scale).astype(BF)
                dv = dv + nn(prob.astype(BF), r["dost"][g, cols])
                dk = dk + nn(ds, r["qst"][g, cols])
                r["dqt"][g, :, cols] += tn(kk, ds)
            acc[g, b, 0] = dk
            acc[g, b, 1] = dv
            if b in (1, 3, 4):
                stage[g, b, 0] = dk.astype(BF)
                stage[g, b, 1] = dv.astype(BF)
            return c

        lax.fori_loop(0, G, body, 0)

    def ret(g, d, to):
        return remote(stage.at[g, d], back.at[g, d], *pair("ret", g, d), to)

    units = [(g, i) for g in range(G) for i in range(2)]

    def far_send(g, i):
        to = prv if (g, i) == (0, 0) else along_y(1)
        return remote(stage.at[g, 4, i], r["relay_back"].at[g, i], *pair("relay_back", g, i), to)

    def far_last(g, i):
        to = prv if (g, i) == (0, 0) else owner
        return remote(r["relay_back"].at[g, i], r["far"].at[g, i], *pair("far", g, i), to)

    def to_peer(d):
        for g in range(G):
            ret(g, d, peer).start()

    def ret4(g):
        @pl.when(core == 1)
        def _():
            ret(g, 3, peer).wait_recv()
            stage[g, 4] = (acc[g, 4] + back[g, 3].astype(F32)).astype(BF)

        for i in range(2):
            far_send(g, i).start()

    def forward_far(g, i):
        far_send(g, i).wait_recv()
        far_last(g, i).start()

    def ret2(g):
        @pl.when(core == 0)
        def _():
            ret(g, 3, peer).wait_recv()

        ret(g, 1, peer).wait_recv()
        t = acc[g, 2] + first_core * back[g, 3].astype(F32) + second_core * back[g, 1].astype(F32)
        stage[g, 2] = t.astype(BF)
        ret(g, 2, prv).start()

    def dkv_copy(g):
        return remote(r["dkv"].at[g], r["dkvp"].at[g], *pair("dkv", g), peer)

    def ret0(g):
        ret(g, 2, prv).wait_recv()
        for i in range(2):
            far_last(g, i).wait_recv()
        t = acc[g, 0] + back[g, 2].astype(F32) + first_core * back[g, 1].astype(F32)
        r["dkv"][g] = (t + r["far"][g].astype(F32)).astype(BF)
        dkv_copy(g).start()

    def made(one, x_first, at, mine, other):
        val = (nn(r["tokt"][core], mine) + nn(r["toktp"][...], other)).astype(BF)
        if x_first:
            one[:, :, at] = val.reshape(X, Y * p.own, val.shape[1])
        else:
            for a in range(X):
                for k in range(Y):
                    ro = (a * Y + k) * p.own
                    one[k, a * p.own : (a + 1) * p.own, at] = val[ro : ro + p.own]

    def made_q(j):
        first, cols, x_first = p.parts[0][j]

        def body(n, c):
            to = pl.ds(pl.multiple_of(n * step, step), step)
            at = pl.ds(pl.multiple_of(first + n * step, step), step)
            made(r[f"one0{j}"], x_first, to, r["dq"][:, at], r["dqp"][:, at])
            return c

        lax.fori_loop(0, cols // step, body, 0)

    def made_kv(j):
        def wide(name):
            return jnp.concatenate([r[name][g, j] for g in range(G)], axis=1)

        made(r[f"one1{j}"], p.parts[1][j][2], slice(0, p.kv_cols), wide("dkv"), wide("dkvp"))

    class Ring:
        def __init__(self, k, i, j):
            x_first = p.parts[i][j][2]
            on_x = x_first == (k == "one")
            self.name = f"{k}{i}{j}"
            self.at, along = (cx, along_x) if on_x else (cy, along_y)
            self.next, self.prev, self.along = along(1), along(R - 1), along

        def chunk(self, o):
            return r[self.name].at[lax.rem(self.at + o, R)]

        def copy(self, k, src, dst, to):
            return remote(src, dst, *pair(self.name, k), to)

        def two_up(self):
            return self.copy(0, self.chunk(2), r[self.name + "up"], self.next)

        def up(self):
            return self.copy(1, self.chunk(1), r[self.name + "left"], self.next)

        def down(self):
            return self.copy(2, self.chunk(R - 1), r[self.name + "right"], self.prev)

        def pass_up(self):
            self.two_up().wait_recv()
            k = lax.rem(self.at + 1, R)
            val = r[self.name][k].astype(F32) + r[self.name + "up"][...].astype(F32)
            r[self.name][k] = val.astype(BF)
            self.up().start()

        def copies(self):
            return [self.two_up(), self.up(), self.down()]

        def total(self):
            self.up().wait_recv()
            self.down().wait_recv()
            t = r[self.name][self.at].astype(F32)
            return t + r[self.name + "left"][...].astype(F32) + r[self.name + "right"][...].astype(F32)

    class Direct(Ring):
        def copies(self):
            for o in range(1, R):
                to = self.along(o)
                yield self.copy(o, self.chunk(o), r[self.name + "got"].at[o - 1], to)

        def start(self):
            for copy in self.copies():
                copy.start()

        def total(self):
            t = r[self.name][self.at].astype(F32)
            for o, copy in enumerate(self.copies()):
                copy.wait_recv()
                t = t + r[self.name + "got"][o].astype(F32)
            return t

    kinds = (Ring, Direct)
    one = [[kinds[i]("one", i, j) for j in range(2)] for i in range(2)]
    two = [[Direct("two", i, j) for j in range(2)] for i in range(2)]

    def start_second(i):
        for j in range(2):
            t = one[i][j].total()
            r[f"two{i}{j}"][...] = t.reshape(R, p.own, t.shape[1]).astype(r[f"two{i}{j}"].dtype)
            two[i][j].start()

    def z_hop(i, o):
        to = lax.rem(z + o, Z)
        s = sm[f"zr{i}"]
        return remote(r[f"zs{i}"].at[to], r[f"zr{i}"].at[o], s.at[0, o], s.at[1, o], me, to)

    def z_gather(i, o):
        to = lax.rem(z + o, Z)
        s = sm[f"zo{i}"]
        return remote(r[f"zo{i}"].at[z], r[f"zo{i}"].at[z], s.at[0, o], s.at[1, o], me, to)

    def loop_z(f):
        def body(k, c):
            f(Z // 2 + (k + 1) // 2 * (1 - 2 * lax.rem(k, 2)))
            return c

        lax.fori_loop(0, Z - 1, body, 0)

    def each_z(f):
        for o in range(1, Z):
            f(o)

    def tiles_of(i):
        per_z = r[f"zs{i}"].shape[1] // 8
        ncb = sum(c for _, c, _ in p.parts[i]) // HEAD
        for t in range(per_z * Z):
            yield t // per_z, (t % per_z) * 8, (t // ncb) * 8, (t % ncb) * HEAD

    def start_z(i):
        pieces = [two[i][j].total() for j in range(2)]
        width = pieces[0].shape[1]
        for zi, zr, ro, co in tiles_of(i):
            part = pieces[co // width]
            co = co % width
            r[f"zs{i}"][zi, zr : zr + 8] = part[ro : ro + 8, co : co + HEAD].astype(BF)
        loop_z(lambda o: z_hop(i, o).start())

    def start_gather(i):
        each_z(lambda o: z_hop(i, o).wait_recv())
        t = r[f"zs{i}"][z].astype(F32)
        for o in range(1, Z):
            t = t + r[f"zr{i}"][o].astype(F32)
        r[f"zo{i}"][z] = (t * ((Z * N * rows) ** -0.5)).astype(r[f"zo{i}"].dtype)
        loop_z(lambda o: z_gather(i, o).start())

    def finish(i):
        each_z(lambda o: z_gather(i, o).wait_recv())
        for zi, zr, ro, co in tiles_of(i):
            val = r[f"zo{i}"][zi, zr : zr + 8].astype(F32)
            if i == 0:
                gq_ref[ro : ro + 8, co : co + HEAD] = val
            elif co < p.kv_cols:
                gk_ref[ro : ro + 8, co : co + HEAD] = val
            else:
                gv_ref[ro : ro + 8, co - p.kv_cols : co - p.kv_cols + HEAD] = val

    z_joined(1, 4)
    mark("grads3", grads, 3)
    to_peer(3)
    mark("grads1", grads, 1)
    to_peer(1)
    mark("grads4", grads, 4)
    mark("ret4", lambda: [ret4(g) for g in range(G)])
    mark("grads2", grads, 2)
    mark("ret2", lambda: [ret2(g) for g in range(G)])
    mark("grads0", grads, 0)

    def dq_rows():
        for n in range(p.heads):
            g, h = divmod(n, p.per)
            r["dq"][:, n * HEAD : (n + 1) * HEAD] = r["dqt"][g, :, h * rows : (h + 1) * rows].T.astype(BF)

    mark("dq_rows", dq_rows)
    dq_copy = remote(r["dq"], r["dqp"], *pair("dq"), peer)
    dq_copy.start()
    def gi_q(n, c):
        at = pl.ds(pl.multiple_of(n * step, step), step)
        r["gi32"][:, at] = nt(r["dq"][...], r["wq"][at])
        return c

    mark("gi_q", lax.fori_loop, 0, p.width // step, gi_q, 0)
    mark("fwd_far", lambda: [forward_far(0, i) for i in range(2)])
    mark("w_dq", lambda: (tokt_copy.wait_recv(), dq_copy.wait_recv()))
    mark("made_q", made_q, 0)
    one[0][0].two_up().start()
    mark("fwd_far2", forward_far, 1, 0)
    mark("made_q", made_q, 1)
    one[0][1].two_up().start()
    mark("fwd_far2", forward_far, 1, 1)

    mark("pass_q", one[0][0].pass_up)
    mark("ret0_0", ret0, 0)
    one[0][0].down().start()
    mark("ret0_1", ret0, 1)
    one[0][1].down().start()
    mark("pass_q", one[0][1].pass_up)
    mark("w_dkv", lambda: [dkv_copy(g).wait_recv() for g in range(G)])
    for j in range(2):
        mark("made_kv", made_kv, j)
        one[1][j].start()

    def gi_kv(n, c):
        at = pl.ds(pl.multiple_of(n * step, step), step)
        val = r["gi32"][:, at]
        for i, w in enumerate(("wk", "wv")):
            for g in range(G):
                val = val + nt(r["dkv"][g, i], r[w][at, g * HEAD : (g + 1) * HEAD])
        gi_ref[:, at] = val.astype(BF)
        return c

    mark("second_0", start_second, 0)
    mark("gi_kv", lax.fori_loop, 0, p.width // step, gi_kv, 0)
    mark("second_1", start_second, 1)
    mark("z_0", start_z, 0)
    mark("z_1", start_z, 1)

    def sent_1():
        for u in range(both):
            h_next(u).wait_send()
        for u in range(G):
            h_four(u).wait_send()
        for copy in (h_one(0), h_three(2), far_one, far_two, tokt_copy, dq_copy):
            copy.wait_send()
        for g in range(G):
            for copy in (ret(g, 3, peer), ret(g, 1, peer), ret(g, 2, prv), dkv_copy(g)):
                copy.wait_send()
        for unit in units:
            far_send(*unit).wait_send()
            far_last(*unit).wait_send()
        for i in range(2):
            for ring_sum in one[i] + two[i]:
                for copy in ring_sum.copies():
                    copy.wait_send()

    mark("sent_1", sent_1)
    mark("gather_0", start_gather, 0)
    mark("gather_1", start_gather, 1)
    mark("sent_2", lambda: [each_z(lambda o, i=i: z_hop(i, o).wait_send()) for i in range(2)])
    mark("finish_0", finish, 0)
    mark("finish_1", finish, 1)

    mark("sent_3", lambda: [each_z(lambda o, i=i: z_gather(i, o).wait_send()) for i in range(2)])


def emit(*refs):
    n = (len(refs) - 1) // 2
    copies = [pltpu.make_async_copy(refs[i], refs[n + i], refs[-1].at[i]) for i in range(n)]
    for c in copies:
        c.start()
    for c in copies:
        c.wait()


def body(sizes, tokens, w_query, key_weight, value_weight, cotangent, segment_ids):
    rows, width = tokens.shape[1:]
    q_cols, kv_cols = w_query.shape[1], key_weight.shape[1]
    p = build_plan(sizes, rows, width, q_cols, kv_cols, segment_ids.shape[1])
    anyspace = pl.BlockSpec(memory_space=pl.ANY)
    vmem = pl.BlockSpec(memory_space=pltpu.VMEM)
    shapes = (
        jax.ShapeDtypeStruct((rows, width), BF),
        jax.ShapeDtypeStruct((p.own, q_cols), F32),
        jax.ShapeDtypeStruct((p.own, kv_cols), F32),
        jax.ShapeDtypeStruct((p.own, kv_cols), F32),
    )
    out = pl.pallas_call(
        functools.partial(kernel, p),
        out_shape=shapes,
        in_specs=[anyspace] * 6,
        out_specs=(vmem,) * 4,
        scratch_shapes=list(p.scratch.values()) + list(p.sems.values()),
        compiler_params=pltpu.CompilerParams(
            collective_id=0, has_side_effects=True, vmem_limit_bytes=VMEM_LIMIT
        ),
        name="step",
    )(tokens[0], w_query, key_weight, value_weight, cotangent[0], segment_ids)
    out = pl.pallas_call(
        emit,
        out_shape=shapes,
        in_specs=[vmem] * 4,
        out_specs=(anyspace,) * 4,
        scratch_shapes=[pltpu.SemaphoreType.DMA((4,))],
        name="emit",
    )(*out)
    return out[0][None], out[1], out[2], out[3]


def solution(mesh):
    sizes = dict(mesh.shape)
    placed = (P("dp", "ctx", None), P(), P(), P(), P("dp", "ctx", None), P("dp", None))
    return jax.shard_map(
        functools.partial(body, sizes),
        mesh=mesh,
        in_specs=placed,
        out_specs=(P("dp", "ctx", None), P("ctx", None), P("ctx", None), P("ctx", None)),
        check_vma=False,
    )
```
